32 devices in a mesh: groups: 2 (over x), seq: 16 (over z, y, core).
Axes of the slice: x: 2, y: 2, z: 4, core: 2. Of those that a mesh axis runs over, the one named last changes fastest.
Arguments:
- bases: int32 [24576], P(('groups', 'seq')), parts along dimension 0, may hold values from 0 to 4
- stem_weight: bfloat16 [5, 4, 768], replicated, may hold values from -3 to 3
- weight_top: bfloat16 [5, 768, 768], P(None, None, 'seq'), may hold values from -0.09375 to 0.09375
- weight_deep: bfloat16 [5, 768, 896], P(None, None, 'seq'), may hold values from -0.09375 to 0.09375
- weight_up: bfloat16 [5, 896, 768], P(None, None, 'seq'), may hold values from -0.09375 to 0.09375
- gain_top: float32 [768], replicated, may hold values from 0.1 to 1.9
- gain_deep: float32 [768], replicated, may hold values from 0.1 to 1.9
- gain_up: float32 [896], replicated, may hold values from 0.1 to 1.9
Outputs:
- decoded: bfloat16 [24576, 768], P(('groups', 'seq')), parts along dimension 0
The draws below stay inside these ranges and needn't reach their ends.
There are 2 independent parts, one for each index of `groups`. The reference program is written for one: setup_inputs(seed, part) draws one part's arguments, and reference() takes and returns one part's arrays. A program takes and returns all parts, laid end to end along the dimension named above; an argument that names none is the same for every part. Nothing has to cross between parts.
Inputs may be any that keep to these rules, and one draw needn't show every extreme that they name: 0 to 3 are the bases A, C, G, T; 4 is an unknown base.
All inputs are finite; a program needn't handle non-finite values.
Results may differ from the reference program's by a relative error of at most 0.008.
Values may be sent and summed in bfloat16 or wider, within the bound.
A program may use at most 128 MiB of HBM per device.

```python
import jax
import jax.numpy as jnp
from jax import lax

C0 = 768
C1 = 896
TAPS = 5
LENGTH = 12288


def with_ends(entries, rng, low, top_value):
    index_at = [jax.random.randint(jax.random.fold_in(rng, axis), (), 0, length) for axis, length in enumerate(entries.shape)]
    widest = entries.shape.index(max(entries.shape))
    next_to = index_at[:widest] + [(index_at[widest] + 1) % entries.shape[widest]] + index_at[widest + 1:]
    return entries.at[tuple(index_at)].set(low).at[tuple(next_to)].set(top_value)


def levels(rng, shape, shards, low, high):
    loudness = 1.0
    for axis_at, shards_of in shards:
        steps = jax.random.uniform(jax.random.fold_in(jax.random.fold_in(rng, 6), axis_at), (shards_of,), jnp.float32, low / len(shards), high / len(shards))
        loudness = loudness * jnp.repeat(jnp.exp(steps), shape[axis_at] // shards_of).reshape((-1,) + (1,) * (len(shape) - 1 - axis_at))
    return loudness


def noise(own_key, shape, width, limit, pieces=(), kind=jnp.bfloat16):
    drawn = width * jax.random.normal(own_key, shape, jnp.float32)
    if pieces:
        drawn = drawn * levels(own_key, shape, pieces, -0.22, 0.18)
    return jnp.clip(drawn, -limit, limit).astype(kind)


def setup_inputs(seed: int = 0, part: int = 0) -> dict:
    keys = jax.random.split(jax.random.key(seed), 9)
    part_keys = jax.random.split(jax.random.fold_in(keys[8], part), 9)
    bases = with_ends(jax.random.randint(part_keys[0], (LENGTH,), 0, 5), jax.random.fold_in(part_keys[0], 1), 0, 4).astype(jnp.int32)
    stem_weight = noise(keys[1], (TAPS, 4, C0), 0.5, 3.0)
    weight_top = noise(keys[2], (TAPS, C0, C0), (TAPS * C0) ** -0.5, 0.09375, ((2, 16),))
    weight_deep = noise(keys[3], (TAPS, C0, C1), (TAPS * C0) ** -0.5, 0.09375, ((2, 16),))
    weight_up = noise(keys[4], (TAPS, C1, C0), (TAPS * C1) ** -0.5, 0.09375, ((2, 16),))
    gain_top = jnp.clip(1.0 + 0.18 * jax.random.normal(keys[5], (C0,), jnp.float32), 0.1, 1.9)
    gain_deep = jnp.clip(1.0 + 0.18 * jax.random.normal(keys[6], (C0,), jnp.float32), 0.1, 1.9)
    gain_up = jnp.clip(1.0 + 0.18 * jax.random.normal(keys[7], (C1,), jnp.float32), 0.1, 1.9)
    return {"bases": bases, "stem_weight": stem_weight, "weight_top": weight_top, "weight_deep": weight_deep, "weight_up": weight_up, "gain_top": gain_top, "gain_deep": gain_deep, "gain_up": gain_up}


def activate(values, gain):
    wide = values.astype(jnp.float32)
    meansq = lax.optimization_barrier(jnp.mean(wide * wide, axis=-1, keepdims=True))
    return jax.nn.gelu(wide * lax.rsqrt(meansq + 1e-06) * gain.astype(jnp.float32)).astype(jnp.bfloat16)

def taps_conv(padded, weight):
    count = padded.shape[0] - weight.shape[0] + 1
    total = jnp.zeros((count, weight.shape[2]), jnp.float32)
    for tap in range(weight.shape[0]):
        total = total + jnp.dot(padded[tap:tap + count], weight[tap], preferred_element_type=jnp.float32)
    return total

def stem_embed(extended, stem_weight, count):
    window = jnp.stack([extended[tap:tap + count] for tap in range(TAPS)], axis=1)
    codes = jnp.arange(1, 5, dtype=jnp.int32)
    onehot = (window[:, :, None] == codes[None, None, :]).astype(jnp.bfloat16).reshape(count, TAPS * 4)
    table = stem_weight.reshape(TAPS * 4, stem_weight.shape[2])
    return jnp.dot(onehot, table, preferred_element_type=jnp.float32)

def reference(bases, stem_weight, weight_top, weight_deep, weight_up, gain_top, gain_deep, gain_up):
    total_len = bases.shape[0]
    extended = jnp.pad(bases + 1, (2, 2))
    embedded = stem_embed(extended, stem_weight, total_len).astype(jnp.bfloat16)
    act_top = jnp.pad(activate(embedded, gain_top), ((2, 2), (0, 0)))
    skip = (embedded.astype(jnp.float32) + taps_conv(act_top, weight_top)).astype(jnp.bfloat16)
    pooled = lax.optimization_barrier(jnp.max(skip.reshape(total_len // 2, 2, skip.shape[1]), axis=1))
    act_deep = jnp.pad(activate(pooled, gain_deep), ((2, 2), (0, 0)))
    widened = jnp.pad(pooled.astype(jnp.float32), ((0, 0), (0, C1 - C0)))
    deep = (taps_conv(act_deep, weight_deep) + widened).astype(jnp.bfloat16)
    raised = jnp.repeat(activate(deep, gain_up), 2, axis=0)
    raised = jnp.pad(raised, ((2, 2), (0, 0)))
    return (taps_conv(raised, weight_up) + skip.astype(jnp.float32)).astype(jnp.bfloat16)
```

```python
import functools

import jax
import jax.numpy as jnp
from jax import lax
from jax.experimental import pallas as pl
from jax.experimental.pallas import tpu as pltpu
from jax.sharding import PartitionSpec as P

TAPS = 5


def with_halo(block, sides, width):
    for axis, dim in sides:
        count = lax.axis_size(axis)
        forward = [(i, i + 1) for i in range(count - 1)]
        backward = [(target, source) for source, target in forward]
        low = lax.ppermute(
            lax.slice_in_dim(block, block.shape[dim] - width, None, axis=dim), axis, forward
        )
        high = lax.ppermute(lax.slice_in_dim(block, 0, width, axis=dim), axis, backward)
        block = jnp.concatenate([low, block, high], axis=dim)
    return block


def activate(values, gain):
    wide = values.astype(jnp.float32)
    meansq = jnp.mean(wide * wide, axis=-1, keepdims=True)
    return jax.nn.gelu(wide * lax.rsqrt(meansq + 1e-06) * gain).astype(jnp.bfloat16)


def taps_conv(padded, weight):
    count = padded.shape[0] - weight.shape[0] + 1
    total = jnp.zeros((count, weight.shape[2]), jnp.float32)
    for tap in range(weight.shape[0]):
        total = total + jnp.dot(
            padded[tap : tap + count], weight[tap], preferred_element_type=jnp.float32
        )
    return total


def stem_embed(extended, stem_weight, count):
    window = jnp.stack([extended[tap : tap + count] for tap in range(TAPS)], axis=1)
    codes = jnp.arange(1, 5, dtype=jnp.int32)
    onehot = (
        (window[:, :, None] == codes[None, None, :]).astype(jnp.bfloat16).reshape(count, TAPS * 4)
    )
    table = stem_weight.reshape(TAPS * 4, stem_weight.shape[2])
    return jnp.dot(onehot, table, preferred_element_type=jnp.float32)


def per_device(
    bases, stem_weight, weight_top, weight_deep, weight_up, gain_top, gain_deep, gain_up
):
    count = bases.shape[0]
    half = count // 2
    full_top = lax.all_gather(weight_top, "seq", axis=2, tiled=True)
    extended = with_halo(bases + 1, (("seq", 0),), 2)
    embedded = stem_embed(extended, stem_weight, count).astype(jnp.bfloat16)
    act_top = with_halo(activate(embedded, gain_top), (("seq", 0),), 2)
    full_deep = lax.all_gather(weight_deep, "seq", axis=2, tiled=True)
    conv_top = taps_conv(act_top, full_top)
    skip = (embedded.astype(jnp.float32) + conv_top).astype(jnp.bfloat16)
    pooled = jnp.max(skip.reshape(half, 2, skip.shape[1]), axis=1)
    act_deep = with_halo(activate(pooled, gain_deep), (("seq", 0),), 2)
    full_up = lax.all_gather(weight_up, "seq", axis=2, tiled=True)
    conv_deep = taps_conv(act_deep, full_deep)
    widened = jnp.pad(
        pooled.astype(jnp.float32), ((0, 0), (0, conv_deep.shape[1] - pooled.shape[1]))
    )
    deep = (conv_deep + widened).astype(jnp.bfloat16)
    act_up = activate(deep, gain_up)
    raised = with_halo(jnp.repeat(act_up, 2, axis=0), (("seq", 0),), 2)
    conv_up = taps_conv(raised, full_up)
    return (conv_up + skip.astype(jnp.float32)).astype(jnp.bfloat16)


MESH = pl.DeviceIdType.MESH
EDGE = 8
CHUNK = 80
LANES = 128
ORDER = (
    "zT", "tab", "e00", "z1e", "e01", "e02", "f020", "f010", "e03", "e04", "f011", "s00", "z1i",
    "s01", "s02", "s03", "s04", "e10", "e11", "e12", "e13", "f021", "cT", "m010", "e14", "s10",
    "m011", "s11", "s12", "f031", "s13", "s14", "nT0", "tn0", "f030", "f110", "m020", "tn1",
    "f120", "m030", "m021", "m031", "z2e", "nT1", "tf0", "f130", "tf1", "m110", "c1", "z2i",
    "pd0", "nD0", "dn0", "f210", "m120", "m130", "pd1", "nD1", "df1", "c2", "dn1", "f220",
    "m210", "df0", "nU0", "f230", "au1", "up10", "m220", "m230", "au0", "nU1", "up01", "up11",
    "up00", "end",
)


def fused_kernel(
    nz,
    half,
    ids_ref,
    stem_ref,
    top_ref,
    deep_ref,
    up_ref,
    gain_top_ref,
    gain_deep_ref,
    gain_up_ref,
    out_ref,
    ids_all,
    ids_wide,
    table,
    table_half,
    full_top,
    full_deep,
    full_up,
    flat_deep,
    both_up,
    wide,
    embedded,
    skip,
    pooled,
    deep,
    result,
    cols_top,
    cols_deep,
    cols_up,
    mixed,
    send_sem,
    recv_sem,
    own_sem,
    ids_sem,
    pair_sem,
):
    g = lax.axis_index("groups")
    s = lax.axis_index("seq")
    core, y, z = s % 2, (s // 2) % 2, s // 4
    members = 4 * nz
    rows = half + 2 * EDGE
    c0 = table.shape[1]
    ch = c0 // 2
    own_refs = (top_ref, deep_ref, up_ref)
    taps_in = tuple(ref.shape[2] for ref in own_refs)
    depths = tuple(ref.shape[1] for ref in own_refs)
    widths = (full_top.shape[1] // 2, full_deep.shape[2] // 2, full_up.shape[1] // 2)
    cut = widths[0] // LANES // 2 * LANES
    parts = (
        ((0, cut), (cut, widths[0] - cut)),
        ((0, widths[1]),),
        ((0, widths[2]),),
    )
    c1 = taps_in[2]

    def index(z_at, y_at, core_at):
        return z_at * 4 + y_at * 2 + core_at

    nearest = [
        sorted(range(nz), key=lambda other: (abs(other - here), other // 2 != here // 2))
        for here in range(nz)
    ]

    def away(k):
        found = jnp.int32(0)
        for here in range(nz):
            found = jnp.where(z == here, nearest[here][k], found)
        return found

    inner = (z > 0) & (z < nz - 1)
    steps = ((z < nz - 1, 1), (z > 0, -1))

    mirror = (1 - g, s)
    across = (g, index(z, 1 - y, core))
    sibling = (g, index(z, y, 1 - core))

    def whole_rows(stage, at):
        n = (at // 4) * 2 + at % 2
        if stage == 1:
            return full_deep.at[n]
        depth = depths[stage]
        ref = full_top if stage == 0 else full_up
        return ref.at[pl.ds(pl.multiple_of(n * depth, 16), depth)]

    own_copies = []
    for stage in range(3):
        copies = []
        for tap in range(TAPS):
            width = taps_in[stage]
            copy = pltpu.make_async_copy(
                own_refs[stage].at[tap],
                whole_rows(stage, s).at[:, pl.ds(tap * width, width)],
                own_sem.at[stage, tap],
            )
            copy.start()
            copies.append(copy)
        own_copies.append(copies)

    def wrap(at):
        return lax.rem(at + members, members)

    def paired(at):
        return index(at // 4, 1 - (at // 2) % 2, at % 2)

    other = paired(s)
    barrier = pltpu.get_barrier_semaphore()
    ids_targets = [
        (wrap(s + 1), wrap(s + 1), 0),
        (wrap(s - 1), wrap(s - 1), 2),
        (paired(wrap(s + 1)), wrap(s + 1), 0),
        (paired(wrap(s - 1)), wrap(s - 1), 2),
        (other, s, 1),
    ]
    partners = [mirror, across, sibling]
    partners += [(g, target) for target, _, _ in ids_targets[:4]]
    partners += [(g, wrap(other + 1)), (g, wrap(other - 1))]
    partners += [(g, index(away(k), y, core)) for k in range(1, nz)]
    for partner in partners:
        pl.semaphore_signal(barrier, inc=1, device_id=partner, device_id_type=MESH)
    pl.semaphore_wait(barrier, len(partners))

    ids_sends = []
    for n, (target, block, slot) in enumerate(ids_targets):
        at_block = (block // 2) % 2
        copy = pltpu.make_async_remote_copy(
            src_ref=ids_ref,
            dst_ref=ids_all.at[at_block, slot],
            send_sem=ids_sem.at[0, n],
            recv_sem=ids_sem.at[1, n],
            device_id=(g, target),
            device_id_type=MESH,
        )
        copy.start()
        ids_sends.append(copy)
    ids_all[y, 1] = ids_ref[...]

    def place(stage, part, h, at):
        low, width = parts[stage][part]
        cols = pl.ds(pl.multiple_of(h * widths[stage] + low, LANES), width)
        return whole_rows(stage, at).at[:, cols]

    started = []

    def send(stage, part, h, at, device, when=True):
        copy = pltpu.make_async_remote_copy(
            src_ref=place(stage, part, h, at),
            dst_ref=place(stage, part, h, at),
            send_sem=send_sem.at[len(started)],
            recv_sem=recv_sem.at[stage, part, h, at],
            device_id=device,
            device_id_type=MESH,
        )
        started.append((copy, when))
        if when is True:
            copy.start()
        else:
            pl.when(when)(copy.start)

    def arrive(stage, part, h, at):
        pltpu.make_async_remote_copy(
            src_ref=place(stage, part, h, at),
            dst_ref=place(stage, part, h, at),
            send_sem=send_sem.at[0],
            recv_sem=recv_sem.at[stage, part, h, at],
            device_id=sibling,
            device_id_type=MESH,
        ).wait_recv()

    def every(stage):
        return range(len(parts[stage]))

    ready = set()

    def loaded(stage):
        if stage not in ready:
            ready.add(stage)
            for copy in own_copies[stage]:
                copy.wait()

    def along_z(stage, which=None):
        loaded(stage)
        for part in every(stage):
            for within, step in steps:
                target = (g, index(jnp.clip(z + step, 0, nz - 1), y, core))
                when = within if which is None else within & which
                send(stage, part, g, s, target, when=when)

    def own_sibling(stage):
        loaded(stage)
        for part in every(stage):
            for h in (g, 1 - g):
                send(stage, part, h, s, sibling)

    def first(stage, k, part):
        far = away(k)
        at = index(far, y, core)
        arrive(stage, part, g, at)
        onward = jnp.where(far < z, z + 1, z - 1)
        send(
            stage,
            part,
            g,
            at,
            (g, index(jnp.clip(onward, 0, nz - 1), y, core)),
            when=(onward >= 0) & (onward < nz),
        )
        send(stage, part, g, at, mirror)
        send(stage, part, g, at, sibling)

    def mirrored(stage, k, part):
        at = index(away(k), y, core)
        arrive(stage, part, 1 - g, at)
        send(stage, part, 1 - g, at, sibling)

    def need(stage, ks):
        loaded(stage)
        for h in (0, 1):
            for k in ks:
                for part in every(stage):
                    arrive(stage, part, h, index(away(k), y, 1 - core))

    chunks = range(0, rows, CHUNK)

    def act_rows(values, gain_ref, start, block):
        meansq = jnp.mean(values * values, axis=-1, keepdims=True)
        result = jax.nn.gelu(values * lax.rsqrt(meansq + 1e-06) * gain_ref[...])
        at = lax.broadcasted_iota(jnp.int32, (values.shape[0], 1), 0) + (
            block * half + start - EDGE
        )
        inside = (at >= 0) & (at < members * half)
        return jnp.where(inside, result, 0.0)

    def member_of(block):
        return index(z, block, core)

    group_top, group_deep, group_up = (4 * depth for depth in depths)

    def prepare_table():
        table[...] = jnp.zeros_like(table)
        for tap in range(TAPS):
            table[tap * 8 : tap * 8 + 4, :] = stem_ref[tap].astype(jnp.float32)
        block = c0 // members * 2
        channel = lax.broadcasted_iota(jnp.int32, (c0, ch), 0)
        local = lax.broadcasted_iota(jnp.int32, (c0, ch), 1)
        wanted = (local // block) * 2 * block + y * block + local % block
        chosen = (channel == wanted).astype(jnp.float32).astype(jnp.bfloat16)
        table_half[...] = jnp.dot(
            table[...].astype(jnp.bfloat16), chosen, preferred_element_type=jnp.float32
        ).astype(jnp.bfloat16)
        wide[...] = jnp.zeros_like(wide)
        across_rows = lax.broadcasted_iota(jnp.int32, (group_deep, c0), 0)
        channel = lax.broadcasted_iota(jnp.int32, (group_deep, c0), 1)
        block = 2 * depths[1]
        for pair in range(2):
            at = (pair * 2 + across_rows // block) * 2 * block + y * block
            same = channel == at + across_rows % block
            flat_deep[pair, :, TAPS * c0 :] = same.astype(jnp.float32).astype(jnp.bfloat16)

    def prepare_ids():
        for copy in ids_sends:
            copy.wait()
        count = 2 * half // LANES
        for block in range(2):
            at = member_of(block)
            for j in range(count + 2):
                if j == 0:
                    row = jnp.where(at > 0, ids_all[block, 0, count - 1 : count, :], 4)
                elif j <= count:
                    row = ids_all[block, 1, j - 1 : j, :]
                else:
                    row = jnp.where(at < members - 1, ids_all[block, 2, 0:1, :], 4)
                ids_wide[block, j * LANES : (j + 1) * LANES, :] = jnp.broadcast_to(
                    row.astype(jnp.float32), (LANES, LANES)
                ).T

    def window(block, parity, start):
        lane = lax.broadcasted_iota(jnp.int32, (CHUNK, LANES), 1)
        picked = jnp.full((CHUNK, LANES), 4.0, jnp.float32)
        for tap in range(TAPS):
            low = LANES + 2 * (start - EDGE) + parity + tap - 2
            moved = ids_wide[block, pl.ds(low, CHUNK, stride=2), :]
            picked = jnp.where(lane // 8 == tap, moved, picked)
        code = jnp.where(lane % 8 < 4, lane % 8, -1).astype(jnp.float32)
        return (picked == code).astype(jnp.float32).astype(jnp.bfloat16)

    def embed(block, start):
        for parity in range(2):
            hot = window(block, parity, start)
            at = parity * rows + start
            local = jnp.dot(
                hot, table_half[...], preferred_element_type=jnp.float32
            ).astype(jnp.bfloat16)
            for pair in range(2):
                embedded[pair, block, at : at + CHUNK, :] = local[
                    :, pair * group_top : (pair + 1) * group_top
                ]
            value = jnp.dot(
                hot, table[...].astype(jnp.bfloat16), preferred_element_type=jnp.float32
            ).astype(jnp.bfloat16)
            result = act_rows(
                value.astype(jnp.float32), gain_top_ref, start, member_of(block)
            )
            wide[parity, EDGE + start : EDGE + start + CHUNK, :c0] = result
            cols_top[
                block, start : start + CHUNK, (2 + parity) * c0 : (3 + parity) * c0
            ] = result.astype(jnp.bfloat16)

    def shift(block, start):
        for parity in range(2):
            for slot, step in ((0, -1), (4, 1)):
                low = EDGE + start + step
                cols_top[
                    block,
                    start : start + CHUNK,
                    (slot + parity) * c0 : (slot + parity + 1) * c0,
                ] = wide[parity, low : low + CHUNK, :c0].astype(jnp.bfloat16)

    def dot_nt(a, b):
        return lax.dot_general(
            a, b, (((1,), (1,)), ((), ())), preferred_element_type=jnp.float32
        )

    near = z // 2
    pairs = (near, 1 - near)
    exchanged = []

    def exchange(stage, n, source, target, when=True):
        copy = pltpu.make_async_remote_copy(
            src_ref=source,
            dst_ref=target,
            send_sem=pair_sem.at[0, stage, n],
            recv_sem=pair_sem.at[1, stage, n],
            device_id=across,
            device_id_type=MESH,
        )
        exchanged.append((copy, when))
        if when is True:
            copy.start()
        else:
            pl.when(when)(copy.start)

    def received(stage, n, target):
        pltpu.make_async_remote_copy(
            src_ref=target,
            dst_ref=target,
            send_sem=pair_sem.at[0, stage, n],
            recv_sem=pair_sem.at[1, stage, n],
            device_id=across,
            device_id_type=MESH,
        ).wait_recv()

    def compute_top(n, block):
        pair = pairs[n]
        weight = full_top[pl.ds(pl.multiple_of(pair * group_top, 16), group_top), :]
        values = []
        for parity in range(2):
            conv = dot_nt(cols_top[block, :, parity * c0 : (parity + TAPS) * c0], weight)
            at = slice(parity * rows, (parity + 1) * rows)
            value = embedded[pair, block, at, :].astype(jnp.float32) + conv
            value = value.astype(jnp.bfloat16).astype(jnp.float32)
            skip[pair, block, :, parity * group_top : (parity + 1) * group_top] = value
            values.append(value)
        pooled[y, pair, block] = jnp.maximum(*values).astype(jnp.bfloat16)
        ref = pooled.at[y, pair, block]
        exchange(0, 2 * n + block, ref, ref)

    def natural(ref, block, start, count, width):
        pieces = []
        for pair in range(2):
            lines = [
                ref[line, pair, block, start : start + count, :].astype(jnp.float32)
                for line in range(2)
            ]
            for low in (0, width):
                pieces += [value[:, low : low + width] for value in lines]
        return jnp.concatenate(pieces, axis=1)

    def prepare_deep(block):
        for n in range(2):
            received(0, 2 * n + block, pooled.at[1 - y, pairs[n], block])
        for start in chunks:
            value = natural(pooled, block, start, CHUNK, group_top // 2)
            cols_deep[block, start : start + CHUNK, TAPS * c0 :] = value.astype(jnp.bfloat16)
            wide[0, EDGE + start : EDGE + start + CHUNK, :c0] = act_rows(
                value, gain_deep_ref, start, member_of(block)
            )
        for start in chunks:
            for tap in range(TAPS):
                low = EDGE + start + tap - 2
                cols_deep[block, start : start + CHUNK, tap * c0 : (tap + 1) * c0] = wide[
                    0, low : low + CHUNK, :c0
                ].astype(jnp.bfloat16)

    def flatten(n):
        depth = depths[1]
        for m in range(4):
            flat_deep[pairs[n], m * depth : (m + 1) * depth, : TAPS * c0] = full_deep[
                pairs[n] * 4 + m
            ]

    def compute_deep(n, block):
        conv = dot_nt(cols_deep[block], flat_deep[pairs[n]])
        deep[y, pairs[n], block] = conv.astype(jnp.bfloat16)
        ref = deep.at[y, pairs[n], block]
        exchange(1, 2 * n + block, ref, ref)

    def prepare_up(block):
        for n in range(2):
            received(1, 2 * n + block, deep.at[1 - y, pairs[n], block])
        for start in chunks:
            value = natural(deep, block, start, CHUNK, group_deep // 2)
            wide[1, EDGE + start : EDGE + start + CHUNK, :] = act_rows(
                value, gain_up_ref, start, member_of(block)
            )
        for start in range(0, half, 96):
            for tap in range(3):
                low = 2 * EDGE + start + tap - 1
                cols_up[block, start : start + 96, tap * c1 : (tap + 1) * c1] = wide[
                    1, low : low + 96, :
                ].astype(jnp.bfloat16)

    def sum_taps(n):
        pair = pairs[n]

        @pl.loop(0, group_up // 16)
        def _(part):
            at = pl.ds(pl.multiple_of(pair * group_up + part * 16, 16), 16)
            taps = [
                full_up[at, tap * c1 : (tap + 1) * c1].astype(jnp.float32)
                for tap in range(TAPS)
            ]
            evens = (taps[0] + taps[1], taps[2] + taps[3], taps[4])
            odds = (taps[0], taps[1] + taps[2], taps[3] + taps[4])
            for parity, sums in enumerate((evens, odds)):
                to = pl.ds(pl.multiple_of(parity * group_up + part * 16, 16), 16)
                for k in range(3):
                    both_up[pair, to, k * c1 : (k + 1) * c1] = sums[k].astype(jnp.bfloat16)

    def compute_up(n, block):
        pair = pairs[n]
        part = half // 2
        for m in range(2):
            at = slice(m * part, (m + 1) * part)
            conv = dot_nt(cols_up[block, at, :], both_up[pair])
            value = conv + skip[pair, block, EDGE + m * part : EDGE + (m + 1) * part, :]
            result[y, block, pair, at, :] = value.astype(jnp.bfloat16)
            ref = result.at[y, block, pair, pl.ds(m * part, part)]
            exchange(2, 4 * block + 2 * n + m, ref, ref, when=y != block)

    def finish():
        part = half // 2
        for block in range(2):
            for n in range(2):
                for m in range(2):
                    ref = result.at[1 - y, block, pairs[n], pl.ds(m * part, part)]
                    pl.when(y == block)(
                        functools.partial(received, 2, 4 * block + 2 * n + m, ref)
                    )
        width = group_up // 2
        tiles = c0 // 2 // LANES
        for pair in range(2):
            for parity in range(2):
                low = parity * group_up
                value = jnp.concatenate(
                    [
                        result[
                            line, y, pair, :, low + piece * width : low + (piece + 1) * width
                        ].astype(jnp.float32)
                        for piece in range(2)
                        for line in range(2)
                    ],
                    axis=1,
                )
                for tile in range(tiles):
                    mixed[tile, pl.ds(parity, half, stride=2), :] = value[
                        :, tile * LANES : (tile + 1) * LANES
                    ]
            for tile in range(tiles):
                low = (pair * tiles + tile) * LANES
                out_ref[:, low : low + LANES] = mixed[tile].astype(jnp.bfloat16)

    ends = jnp.logical_not(inner)
    others = range(1, nz)
    todo = {
        "tab": lambda: (prepare_table(), prepare_ids()),
        "zT": lambda: along_z(0),
        "cT": lambda: own_sibling(0),
        "c1": lambda: own_sibling(1),
        "c2": lambda: own_sibling(2),
        "z1e": lambda: along_z(1, ends),
        "z1i": lambda: along_z(1, inner),
        "z2e": lambda: along_z(2, ends),
        "z2i": lambda: along_z(2, inner),
        "nT0": lambda: need(0, [0, 1]),
        "nT1": lambda: need(0, others[1:]),
        "nD0": lambda: (need(1, [0, 1]), flatten(0)),
        "nD1": lambda: (need(1, others[1:]), flatten(1)),
        "nU0": lambda: (need(2, [0, 1]), sum_taps(0)),
        "nU1": lambda: (need(2, others[1:]), sum_taps(1)),
        "end": finish,
    }
    for b in range(2):
        for i, start in enumerate(chunks):
            todo[f"e{b}{i}"] = functools.partial(embed, b, start)
            todo[f"s{b}{i}"] = functools.partial(shift, b, start)
        for n, letter in enumerate("nf"):
            todo[f"t{letter}{b}"] = functools.partial(compute_top, n, b)
            todo[f"d{letter}{b}"] = functools.partial(compute_deep, n, b)
            todo[f"up{b}{n}"] = functools.partial(compute_up, n, b)
        todo[f"pd{b}"] = functools.partial(prepare_deep, b)
        todo[f"au{b}"] = functools.partial(prepare_up, b)
    for stage in range(3):
        for k in others:
            for part in every(stage):
                todo[f"f{stage}{k}{part}"] = functools.partial(first, stage, k, part)
                todo[f"m{stage}{k}{part}"] = functools.partial(mirrored, stage, k, part)
    for name in ORDER:
        todo.pop(name)()
    assert not todo
    for copy, when in started + exchanged:
        if when is True:
            copy.wait_send()
        else:
            pl.when(when)(copy.wait_send)


def fused_device(
    bases, stem_weight, weight_top, weight_deep, weight_up, gain_top, gain_deep, gain_up
):
    count = bases.shape[0]
    half = count // 2
    rows = half + 2 * EDGE
    members = lax.axis_size("seq")
    nz = members // 4
    c0 = stem_weight.shape[2]
    c1 = weight_up.shape[1]
    ch = c0 // 2
    bf16, f32 = jnp.bfloat16, jnp.float32

    shards = [weight.transpose(0, 2, 1) for weight in (weight_top, weight_deep, weight_up)]
    lines = bases.reshape(-1, LANES)
    ids = jnp.pad(lines, ((0, -lines.shape[0] % 8), (0, 0)))

    k0, k1, k2 = (TAPS * shard.shape[2] for shard in shards)
    k2 += -k2 % 256
    line = members // 2
    top, deep, up = (4 * shard.shape[1] for shard in shards)
    pieces = (2, 1, 1)
    sends = sum(pieces) * (4 + 2 + (nz - 1) * 4)
    out = pl.pallas_call(
        functools.partial(fused_kernel, nz, half),
        out_shape=jax.ShapeDtypeStruct((count, c0), bf16),
        in_specs=[pl.BlockSpec(memory_space=pltpu.VMEM)] * 2
        + [pl.BlockSpec(memory_space=pl.ANY)] * 3
        + [pl.BlockSpec(memory_space=pltpu.VMEM)] * 3,
        out_specs=pl.BlockSpec(memory_space=pltpu.VMEM),
        scratch_shapes=[
            pltpu.VMEM((2, 3) + ids.shape, jnp.int32),
            pltpu.VMEM((2, count + 2 * LANES, LANES), f32),
            pltpu.VMEM((LANES, c0), f32),
            pltpu.VMEM((LANES, ch), bf16),
            pltpu.VMEM((ch, k0), bf16),
            pltpu.VMEM((line, weight_deep.shape[2], k1), bf16),
            pltpu.VMEM((ch, k2), bf16),
            pltpu.VMEM((2, deep, k1 + c0), bf16),
            pltpu.VMEM((2, 2 * up, 3 * c1), bf16),
            pltpu.VMEM((2, rows + 2 * EDGE, c1), f32),
            pltpu.VMEM((2, 2, 2 * rows, top), bf16),
            pltpu.VMEM((2, 2, rows, 2 * top), f32),
            pltpu.VMEM((2, 2, 2, rows, top), bf16),
            pltpu.VMEM((2, 2, 2, rows, deep), bf16),
            pltpu.VMEM((2, 2, 2, half, 2 * up), bf16),
            pltpu.VMEM((2, rows, 6 * c0), bf16),
            pltpu.VMEM((2, rows, k1 + c0), bf16),
            pltpu.VMEM((2, half, 3 * c1), bf16),
            pltpu.VMEM((ch // LANES, count, LANES), f32),
            pltpu.SemaphoreType.DMA((sends,)),
            pltpu.SemaphoreType.DMA((3, max(pieces), 2, members)),
            pltpu.SemaphoreType.DMA((3, TAPS)),
            pltpu.SemaphoreType.DMA((2, 5)),
            pltpu.SemaphoreType.DMA((2, 3, 8)),
        ],
        compiler_params=pltpu.CompilerParams(
            collective_id=0, has_side_effects=True, vmem_limit_bytes=67043328
        ),
    )(
        ids,
        stem_weight,
        *shards,
        gain_top,
        gain_deep,
        gain_up,
    )
    return out


def solution(mesh):
    members = mesh.shape["seq"]

    def device_step(*args):
        bases, stem_weight, weight_top, _, weight_up, *_ = args
        fits = (
            mesh.shape["groups"] == 2
            and members % 4 == 0
            and members == 16
            and weight_top.shape[2] % 16 == 0
            and weight_up.shape[2] % 16 == 0
            and stem_weight.shape[2] % 256 == 0
            and (bases.shape[0] // 2 + 2 * EDGE) % CHUNK == 0
            and bases.shape[0] % 192 == 0
            and bases.shape[0] % LANES == 0
        )
        return (fused_device if fits else per_device)(*args)

    placed = (
        P(("groups", "seq")),
        P(),
        P(None, None, "seq"),
        P(None, None, "seq"),
        P(None, None, "seq"),
        P(),
        P(),
        P(),
    )
    return jax.shard_map(
        device_step,
        mesh=mesh,
        in_specs=placed,
        out_specs=P(("groups", "seq"), None),
        check_vma=False,
    )
```

```python
import functools

import jax
import jax.numpy as jnp
from jax import lax
from jax.experimental import pallas as pl
from jax.experimental.pallas import tpu as pltpu
from jax.sharding import PartitionSpec as P

TAPS = 5


def with_halo(block, sides, width):
    for axis, dim in sides:
        count = lax.axis_size(axis)
        forward = [(i, i + 1) for i in range(count - 1)]
        backward = [(target, source) for source, target in forward]
        low = lax.ppermute(
            lax.slice_in_dim(block, block.shape[dim] - width, None, axis=dim), axis, forward
        )
        high = lax.ppermute(lax.slice_in_dim(block, 0, width, axis=dim), axis, backward)
        block = jnp.concatenate([low, block, high], axis=dim)
    return block


def activate(values, gain):
    wide = values.astype(jnp.float32)
    meansq = jnp.mean(wide * wide, axis=-1, keepdims=True)
    return jax.nn.gelu(wide * lax.rsqrt(meansq + 1e-06) * gain).astype(jnp.bfloat16)


def taps_conv(padded, weight):
    count = padded.shape[0] - weight.shape[0] + 1
    total = jnp.zeros((count, weight.shape[2]), jnp.float32)
    for tap in range(weight.shape[0]):
        total = total + jnp.dot(
            padded[tap : tap + count], weight[tap], preferred_element_type=jnp.float32
        )
    return total


def stem_embed(extended, stem_weight, count):
    window = jnp.stack([extended[tap : tap + count] for tap in range(TAPS)], axis=1)
    codes = jnp.arange(1, 5, dtype=jnp.int32)
    onehot = (
        (window[:, :, None] == codes[None, None, :]).astype(jnp.bfloat16).reshape(count, TAPS * 4)
    )
    table = stem_weight.reshape(TAPS * 4, stem_weight.shape[2])
    return jnp.dot(onehot, table, preferred_element_type=jnp.float32)


def per_device(
    bases, stem_weight, weight_top, weight_deep, weight_up, gain_top, gain_deep, gain_up
):
    count = bases.shape[0]
    half = count // 2
    full_top = lax.all_gather(weight_top, "seq", axis=2, tiled=True)
    extended = with_halo(bases + 1, (("seq", 0),), 2)
    embedded = stem_embed(extended, stem_weight, count).astype(jnp.bfloat16)
    act_top = with_halo(activate(embedded, gain_top), (("seq", 0),), 2)
    full_deep = lax.all_gather(weight_deep, "seq", axis=2, tiled=True)
    conv_top = taps_conv(act_top, full_top)
    skip = (embedded.astype(jnp.float32) + conv_top).astype(jnp.bfloat16)
    pooled = jnp.max(skip.reshape(half, 2, skip.shape[1]), axis=1)
    act_deep = with_halo(activate(pooled, gain_deep), (("seq", 0),), 2)
    full_up = lax.all_gather(weight_up, "seq", axis=2, tiled=True)
    conv_deep = taps_conv(act_deep, full_deep)
    widened = jnp.pad(
        pooled.astype(jnp.float32), ((0, 0), (0, conv_deep.shape[1] - pooled.shape[1]))
    )
    deep = (conv_deep + widened).astype(jnp.bfloat16)
    act_up = activate(deep, gain_up)
    raised = with_halo(jnp.repeat(act_up, 2, axis=0), (("seq", 0),), 2)
    conv_up = taps_conv(raised, full_up)
    return (conv_up + skip.astype(jnp.float32)).astype(jnp.bfloat16)


MESH = pl.DeviceIdType.MESH
EDGE = 8
CHUNK = 80
LANES = 128
PARTS = (2, 1, 1)
ORDER = (
    "zT", "tab", "f010", "e00", "e01", "e02", "e03", "f011", "e04", "s00", "f021", "s01", "s02",
    "s03", "cT", "s04", "e10", "z1e", "e11", "e12", "e13", "e14", "f030", "m010", "s10", "m011",
    "s11", "s12", "s13", "f031", "s14", "nT0", "tn0", "f020", "z1i", "m021", "z2e", "tn1",
    "m031", "c2", "m030", "m020", "f110", "nT1", "tf0", "f120", "tf1", "c1", "m110", "f130",
    "nD0", "z2i", "pd0", "dn0", "pd1", "f210", "dn1", "m130", "m120", "f220", "nD1", "df1",
    "df0", "m210", "f230", "nU0", "au1", "up10", "m220", "au0", "m230", "up00", "nU1", "up11",
    "up01", "end0", "end1",
)


def fused_kernel(
    nz,
    half,
    ids_ref,
    stem_ref,
    top_ref,
    deep_ref,
    up_ref,
    gain_top_ref,
    gain_deep_ref,
    gain_up_ref,
    out_ref,
    ids_all,
    ids_wide,
    table,
    table_half,
    full_top,
    full_deep,
    full_up,
    flat_deep,
    both_up,
    wide,
    embedded,
    skip,
    pooled,
    deep,
    result,
    cols_top,
    cols_deep,
    cols_up,
    mixed,
    send_sem,
    recv_sem,
    own_sem,
    ids_sem,
    pair_sem,
):
    g = lax.axis_index("groups")
    s = lax.axis_index("seq")
    core, y, z = s % 2, (s // 2) % 2, s // 4
    members = 4 * nz
    rows = half + 2 * EDGE
    c0 = table.shape[1]
    ch = c0 // 2
    own_refs = (top_ref, deep_ref, up_ref)
    taps_in = tuple(ref.shape[2] for ref in own_refs)
    depths = tuple(ref.shape[1] for ref in own_refs)
    widths = (full_top.shape[1] // 2, full_deep.shape[2] // 2, full_up.shape[1] // 2)
    parts = []
    for width, count in zip(widths, PARTS):
        cuts = [width // LANES * n // count * LANES for n in range(count + 1)]
        parts.append([(low, high - low) for low, high in zip(cuts, cuts[1:])])
    c1 = taps_in[2]

    def index(z_at, y_at, core_at):
        return z_at * 4 + y_at * 2 + core_at

    nearest = [
        sorted(range(nz), key=lambda other: (abs(other - here), other // 2 != here // 2))
        for here in range(nz)
    ]

    def away(k):
        found = jnp.int32(0)
        for here in range(nz):
            found = jnp.where(z == here, nearest[here][k], found)
        return found

    inner = (z > 0) & (z < nz - 1)
    steps = ((z < nz - 1, 1), (z > 0, -1))

    mirror = (1 - g, s)
    across = (g, index(z, 1 - y, core))
    sibling = (g, index(z, y, 1 - core))

    def whole_rows(stage, at):
        n = (at // 4) * 2 + at % 2
        if stage == 1:
            return full_deep.at[n]
        depth = depths[stage]
        ref = full_top if stage == 0 else full_up
        return ref.at[pl.ds(pl.multiple_of(n * depth, 16), depth)]

    own_copies = []
    for stage in range(3):
        copies = []
        for tap in range(TAPS):
            width = taps_in[stage]
            copy = pltpu.make_async_copy(
                own_refs[stage].at[tap],
                whole_rows(stage, s).at[:, pl.ds(tap * width, width)],
                own_sem.at[stage, tap],
            )
            copy.start()
            copies.append(copy)
        own_copies.append(copies)

    def paired(at):
        return index(at // 4, 1 - (at // 2) % 2, at % 2)

    def inside(at):
        return (at >= 0) & (at < members)

    def device(at):
        return (g, jnp.clip(at, 0, members - 1))

    other = paired(s)
    ids_targets = [
        (s + 1, s + 1, 0),
        (s - 1, s - 1, 2),
        (paired(s + 1), s + 1, 0),
        (paired(s - 1), s - 1, 2),
        (other, s, 1),
    ]
    partners = [(mirror, True), (across, True), (sibling, True)]
    partners += [(device(at), inside(block)) for at, block, _ in ids_targets[:4]]
    partners += [(device(at), inside(at)) for at in (other - 1, other + 1)]
    partners += [
        ((g, index(jnp.clip(z + step, 0, nz - 1), y, core)), within)
        for within, step in steps
    ]
    barrier = pltpu.get_barrier_semaphore()
    count = 0
    for partner, when in partners:
        signal = functools.partial(
            pl.semaphore_signal, barrier, inc=1, device_id=partner, device_id_type=MESH
        )
        if when is True:
            signal()
            count = count + 1
        else:
            pl.when(when)(signal)
            count = count + when.astype(jnp.int32)
    pl.semaphore_wait(barrier, count)

    ids_moves = []
    for n, (target, block, slot) in enumerate(ids_targets):
        when = inside(block)
        copy = pltpu.make_async_remote_copy(
            src_ref=ids_ref,
            dst_ref=ids_all.at[jnp.clip(block, 0, members - 1) // 2 % 2, slot],
            send_sem=ids_sem.at[0, n],
            recv_sem=ids_sem.at[1, n],
            device_id=device(target),
            device_id_type=MESH,
        )
        pl.when(when)(copy.start)
        ids_moves.append((copy, when))
    ids_all[y, 1] = ids_ref[...]

    def ids_ready():
        arriving = (
            inside(s - 1),
            inside(s + 1),
            inside(other - 1),
            inside(other + 1),
            other >= 0,
        )
        for (copy, when), comes in zip(ids_moves, arriving):
            pl.when(when)(copy.wait_send)
            pl.when(comes)(copy.wait_recv)

    def place(stage, part, h, at):
        low, width = parts[stage][part]
        cols = pl.ds(pl.multiple_of(h * widths[stage] + low, LANES), width)
        return whole_rows(stage, at).at[:, cols]

    started = []

    def send(stage, part, h, at, device, when=True):
        copy = pltpu.make_async_remote_copy(
            src_ref=place(stage, part, h, at),
            dst_ref=place(stage, part, h, at),
            send_sem=send_sem.at[len(started)],
            recv_sem=recv_sem.at[stage, part, h, at],
            device_id=device,
            device_id_type=MESH,
        )
        started.append((copy, when))
        if when is True:
            copy.start()
        else:
            pl.when(when)(copy.start)

    def arrive(stage, part, h, at):
        pltpu.make_async_remote_copy(
            src_ref=place(stage, part, h, at),
            dst_ref=place(stage, part, h, at),
            send_sem=send_sem.at[0],
            recv_sem=recv_sem.at[stage, part, h, at],
            device_id=sibling,
            device_id_type=MESH,
        ).wait_recv()

    def every(stage):
        return range(len(parts[stage]))

    ready = set()

    def loaded(stage):
        if stage not in ready:
            ready.add(stage)
            for copy in own_copies[stage]:
                copy.wait()

    def along_z(stage, which=None):
        loaded(stage)
        for part in every(stage):
            for within, step in steps:
                target = (g, index(jnp.clip(z + step, 0, nz - 1), y, core))
                when = within if which is None else within & which
                send(stage, part, g, s, target, when=when)

    def own_sibling(stage):
        loaded(stage)
        for part in every(stage):
            for h in (g, 1 - g):
                send(stage, part, h, s, sibling)

    def first(stage, k, part):
        far = away(k)
        at = index(far, y, core)
        arrive(stage, part, g, at)
        onward = jnp.where(far < z, z + 1, z - 1)
        send(
            stage,
            part,
            g,
            at,
            (g, index(jnp.clip(onward, 0, nz - 1), y, core)),
            when=(onward >= 0) & (onward < nz),
        )
        send(stage, part, g, at, mirror)
        send(stage, part, g, at, sibling)

    def mirrored(stage, k, part):
        at = index(away(k), y, core)
        arrive(stage, part, 1 - g, at)
        send(stage, part, 1 - g, at, sibling)

    def need(stage, ks):
        loaded(stage)
        for h in (0, 1):
            for k in ks:
                for part in every(stage):
                    arrive(stage, part, h, index(away(k), y, 1 - core))

    chunks = range(0, rows, CHUNK)

    def act_rows(values, gain_ref, start, block):
        meansq = jnp.mean(values * values, axis=-1, keepdims=True)
        result = jax.nn.gelu(values * lax.rsqrt(meansq + 1e-06) * gain_ref[...])
        at = lax.broadcasted_iota(jnp.int32, (values.shape[0], 1), 0) + (
            block * half + start - EDGE
        )
        inside = (at >= 0) & (at < members * half)
        return jnp.where(inside, result, 0.0)

    def member_of(block):
        return index(z, block, core)

    group_top, group_deep, group_up = (4 * depth for depth in depths)

    def prepare_table():
        table[...] = jnp.zeros_like(table)
        for tap in range(TAPS):
            table[tap * 8 : tap * 8 + 4, :] = stem_ref[tap].astype(jnp.float32)
        block = c0 // members * 2
        channel = lax.broadcasted_iota(jnp.int32, (c0, ch), 0)
        local = lax.broadcasted_iota(jnp.int32, (c0, ch), 1)
        wanted = (local // block) * 2 * block + y * block + local % block
        chosen = (channel == wanted).astype(jnp.float32).astype(jnp.bfloat16)
        table_half[...] = jnp.dot(
            table[...].astype(jnp.bfloat16), chosen, preferred_element_type=jnp.float32
        ).astype(jnp.bfloat16)
        wide[...] = jnp.zeros_like(wide)
        across_rows = lax.broadcasted_iota(jnp.int32, (group_deep, c0), 0)
        channel = lax.broadcasted_iota(jnp.int32, (group_deep, c0), 1)
        block = 2 * depths[1]
        for pair in range(2):
            at = (pair * 2 + across_rows // block) * 2 * block + y * block
            same = channel == at + across_rows % block
            flat_deep[pair, :, TAPS * c0 :] = same.astype(jnp.float32).astype(jnp.bfloat16)

    def prepare_ids():
        ids_ready()
        count = 2 * half // LANES
        for block in range(2):
            at = member_of(block)
            for j in range(count + 2):
                if j == 0:
                    row = jnp.where(at > 0, ids_all[block, 0, count - 1 : count, :], 4)
                elif j <= count:
                    row = ids_all[block, 1, j - 1 : j, :]
                else:
                    row = jnp.where(at < members - 1, ids_all[block, 2, 0:1, :], 4)
                ids_wide[block, j * LANES : (j + 1) * LANES, :] = jnp.broadcast_to(
                    row.astype(jnp.float32), (LANES, LANES)
                ).T

    def window(block, parity, start):
        lane = lax.broadcasted_iota(jnp.int32, (CHUNK, LANES), 1)
        picked = jnp.full((CHUNK, LANES), 4.0, jnp.float32)
        for tap in range(TAPS):
            low = LANES + 2 * (start - EDGE) + parity + tap - 2
            moved = ids_wide[block, pl.ds(low, CHUNK, stride=2), :]
            picked = jnp.where(lane // 8 == tap, moved, picked)
        code = jnp.where(lane % 8 < 4, lane % 8, -1).astype(jnp.float32)
        return (picked == code).astype(jnp.float32).astype(jnp.bfloat16)

    def embed(block, start):
        for parity in range(2):
            hot = window(block, parity, start)
            at = parity * rows + start
            local = jnp.dot(
                hot, table_half[...], preferred_element_type=jnp.float32
            ).astype(jnp.bfloat16)
            for pair in range(2):
                embedded[pair, block, at : at + CHUNK, :] = local[
                    :, pair * group_top : (pair + 1) * group_top
                ]
            value = jnp.dot(
                hot, table[...].astype(jnp.bfloat16), preferred_element_type=jnp.float32
            ).astype(jnp.bfloat16)
            result = act_rows(
                value.astype(jnp.float32), gain_top_ref, start, member_of(block)
            )
            wide[parity, EDGE + start : EDGE + start + CHUNK, :c0] = result
            cols_top[
                block, start : start + CHUNK, (2 + parity) * c0 : (3 + parity) * c0
            ] = result.astype(jnp.bfloat16)

    def shift(block, start):
        for parity in range(2):
            for slot, step in ((0, -1), (4, 1)):
                low = EDGE + start + step
                cols_top[
                    block,
                    start : start + CHUNK,
                    (slot + parity) * c0 : (slot + parity + 1) * c0,
                ] = wide[parity, low : low + CHUNK, :c0].astype(jnp.bfloat16)

    def dot_nt(a, b):
        return lax.dot_general(
            a, b, (((1,), (1,)), ((), ())), preferred_element_type=jnp.float32
        )

    near = z // 2
    pairs = (near, 1 - near)
    exchanged = []

    def exchange(stage, n, source, target, when=True):
        copy = pltpu.make_async_remote_copy(
            src_ref=source,
            dst_ref=target,
            send_sem=pair_sem.at[0, stage, n],
            recv_sem=pair_sem.at[1, stage, n],
            device_id=across,
            device_id_type=MESH,
        )
        exchanged.append((copy, when))
        if when is True:
            copy.start()
        else:
            pl.when(when)(copy.start)

    def received(stage, n, target):
        pltpu.make_async_remote_copy(
            src_ref=target,
            dst_ref=target,
            send_sem=pair_sem.at[0, stage, n],
            recv_sem=pair_sem.at[1, stage, n],
            device_id=across,
            device_id_type=MESH,
        ).wait_recv()

    def compute_top(n, block):
        pair = pairs[n]
        weight = full_top[pl.ds(pl.multiple_of(pair * group_top, 16), group_top), :]
        values = []
        for parity in range(2):
            conv = dot_nt(cols_top[block, :, parity * c0 : (parity + TAPS) * c0], weight)
            at = slice(parity * rows, (parity + 1) * rows)
            value = embedded[pair, block, at, :].astype(jnp.float32) + conv
            value = value.astype(jnp.bfloat16).astype(jnp.float32)
            skip[pair, block, :, parity * group_top : (parity + 1) * group_top] = value
            values.append(value)
        pooled[y, pair, block] = jnp.maximum(*values).astype(jnp.bfloat16)
        ref = pooled.at[y, pair, block]
        exchange(0, 2 * n + block, ref, ref)

    def natural(ref, block, start, count, width):
        pieces = []
        for pair in range(2):
            lines = [
                ref[line, pair, block, start : start + count, :].astype(jnp.float32)
                for line in range(2)
            ]
            for low in (0, width):
                pieces += [value[:, low : low + width] for value in lines]
        return jnp.concatenate(pieces, axis=1)

    def prepare_deep(block):
        for n in range(2):
            received(0, 2 * n + block, pooled.at[1 - y, pairs[n], block])
        for start in chunks:
            value = natural(pooled, block, start, CHUNK, group_top // 2)
            cols_deep[block, start : start + CHUNK, TAPS * c0 :] = value.astype(jnp.bfloat16)
            wide[0, EDGE + start : EDGE + start + CHUNK, :c0] = act_rows(
                value, gain_deep_ref, start, member_of(block)
            )
        for start in chunks:
            for tap in range(TAPS):
                low = EDGE + start + tap - 2
                cols_deep[block, start : start + CHUNK, tap * c0 : (tap + 1) * c0] = wide[
                    0, low : low + CHUNK, :c0
                ].astype(jnp.bfloat16)

    def flatten(n):
        depth = depths[1]
        for m in range(4):
            flat_deep[pairs[n], m * depth : (m + 1) * depth, : TAPS * c0] = full_deep[
                pairs[n] * 4 + m
            ]

    def compute_deep(n, block):
        conv = dot_nt(cols_deep[block], flat_deep[pairs[n]])
        deep[y, pairs[n], block] = conv.astype(jnp.bfloat16)
        ref = deep.at[y, pairs[n], block]
        exchange(1, 2 * n + block, ref, ref)

    def prepare_up(block):
        for n in range(2):
            received(1, 2 * n + block, deep.at[1 - y, pairs[n], block])
        for start in chunks:
            value = natural(deep, block, start, CHUNK, group_deep // 2)
            wide[1, EDGE + start : EDGE + start + CHUNK, :] = act_rows(
                value, gain_up_ref, start, member_of(block)
            )
        for start in range(0, half, 96):
            for tap in range(3):
                low = 2 * EDGE + start + tap - 1
                cols_up[block, start : start + 96, tap * c1 : (tap + 1) * c1] = wide[
                    1, low : low + 96, :
                ].astype(jnp.bfloat16)

    def sum_taps(n):
        pair = pairs[n]

        @pl.loop(0, group_up // 16)
        def _(part):
            at = pl.ds(pl.multiple_of(pair * group_up + part * 16, 16), 16)
            taps = [
                full_up[at, tap * c1 : (tap + 1) * c1].astype(jnp.float32)
                for tap in range(TAPS)
            ]
            evens = (taps[0] + taps[1], taps[2] + taps[3], taps[4])
            odds = (taps[0], taps[1] + taps[2], taps[3] + taps[4])
            for parity, sums in enumerate((evens, odds)):
                to = pl.ds(pl.multiple_of(parity * group_up + part * 16, 16), 16)
                for k in range(3):
                    both_up[pair, to, k * c1 : (k + 1) * c1] = sums[k].astype(jnp.bfloat16)

    def compute_up(n, block):
        pair = pairs[n]
        part = half // 2
        for m in range(2):
            at = slice(m * part, (m + 1) * part)
            conv = dot_nt(cols_up[block, at, :], both_up[pair])
            value = conv + skip[pair, block, EDGE + m * part : EDGE + (m + 1) * part, :]
            result[y, block, pair, at, :] = value.astype(jnp.bfloat16)
            ref = result.at[y, block, pair, pl.ds(m * part, part)]
            exchange(2, 4 * block + 2 * n + m, ref, ref, when=y != block)

    def finish(n):
        part = half // 2
        pair = pairs[n]
        for block in range(2):
            for m in range(2):
                ref = result.at[1 - y, block, pair, pl.ds(m * part, part)]
                pl.when(y == block)(
                    functools.partial(received, 2, 4 * block + 2 * n + m, ref)
                )
        width = group_up // 2
        tiles = c0 // 2 // LANES
        for parity in range(2):
            low = parity * group_up
            value = jnp.concatenate(
                [
                    result[
                        line, y, pair, :, low + piece * width : low + (piece + 1) * width
                    ].astype(jnp.float32)
                    for piece in range(2)
                    for line in range(2)
                ],
                axis=1,
            )
            for tile in range(tiles):
                mixed[tile, pl.ds(parity, half, stride=2), :] = value[
                    :, tile * LANES : (tile + 1) * LANES
                ]
        for tile in range(tiles):
            low = pl.multiple_of((pair * tiles + tile) * LANES, LANES)
            out_ref[:, pl.ds(low, LANES)] = mixed[tile].astype(jnp.bfloat16)

    ends = jnp.logical_not(inner)
    others = range(1, nz)
    todo = {
        "tab": lambda: (prepare_table(), prepare_ids()),
        "zT": lambda: along_z(0),
        "cT": lambda: own_sibling(0),
        "c1": lambda: own_sibling(1),
        "c2": lambda: own_sibling(2),
        "z1e": lambda: along_z(1, ends),
        "z1i": lambda: along_z(1, inner),
        "z2e": lambda: along_z(2, ends),
        "z2i": lambda: along_z(2, inner),
        "nT0": lambda: need(0, [0, 1]),
        "nT1": lambda: need(0, others[1:]),
        "nD0": lambda: (need(1, [0, 1]), flatten(0)),
        "nD1": lambda: (need(1, others[1:]), flatten(1)),
        "nU0": lambda: (need(2, [0, 1]), sum_taps(0)),
        "nU1": lambda: (need(2, others[1:]), sum_taps(1)),
        "end0": lambda: finish(0),
        "end1": lambda: finish(1),
    }
    for b in range(2):
        for i, start in enumerate(chunks):
            todo[f"e{b}{i}"] = functools.partial(embed, b, start)
            todo[f"s{b}{i}"] = functools.partial(shift, b, start)
        for n, letter in enumerate("nf"):
            todo[f"t{letter}{b}"] = functools.partial(compute_top, n, b)
            todo[f"d{letter}{b}"] = functools.partial(compute_deep, n, b)
            todo[f"up{b}{n}"] = functools.partial(compute_up, n, b)
        todo[f"pd{b}"] = functools.partial(prepare_deep, b)
        todo[f"au{b}"] = functools.partial(prepare_up, b)
    for stage in range(3):
        for k in others:
            for part in every(stage):
                todo[f"f{stage}{k}{part}"] = functools.partial(first, stage, k, part)
                todo[f"m{stage}{k}{part}"] = functools.partial(mirrored, stage, k, part)
    for name in ORDER:
        todo.pop(name)()
    assert not todo
    for copy, when in started + exchanged:
        if when is True:
            copy.wait_send()
        else:
            pl.when(when)(copy.wait_send)


def fused_device(
    bases, stem_weight, weight_top, weight_deep, weight_up, gain_top, gain_deep, gain_up
):
    count = bases.shape[0]
    half = count // 2
    rows = half + 2 * EDGE
    members = lax.axis_size("seq")
    nz = members // 4
    c0 = stem_weight.shape[2]
    c1 = weight_up.shape[1]
    ch = c0 // 2
    bf16, f32 = jnp.bfloat16, jnp.float32

    shards = [weight.transpose(0, 2, 1) for weight in (weight_top, weight_deep, weight_up)]
    ids = bases.reshape(-1, LANES)

    k0, k1, k2 = (TAPS * shard.shape[2] for shard in shards)
    k2 += -k2 % 256
    line = members // 2
    top, deep, up = (4 * shard.shape[1] for shard in shards)
    pieces = PARTS
    sends = sum(pieces) * (4 + 2 + (nz - 1) * 4)
    out = pl.pallas_call(
        functools.partial(fused_kernel, nz, half),
        out_shape=jax.ShapeDtypeStruct((count, c0), bf16),
        in_specs=[pl.BlockSpec(memory_space=pltpu.VMEM)] * 2
        + [pl.BlockSpec(memory_space=pl.ANY)] * 3
        + [pl.BlockSpec(memory_space=pltpu.VMEM)] * 3,
        out_specs=pl.BlockSpec(memory_space=pltpu.VMEM),
        scratch_shapes=[
            pltpu.VMEM((2, 3) + ids.shape, jnp.int32),
            pltpu.VMEM((2, count + 2 * LANES, LANES), f32),
            pltpu.VMEM((LANES, c0), f32),
            pltpu.VMEM((LANES, ch), bf16),
            pltpu.VMEM((ch, k0), bf16),
            pltpu.VMEM((line, weight_deep.shape[2], k1), bf16),
            pltpu.VMEM((ch, k2), bf16),
            pltpu.VMEM((2, deep, k1 + c0), bf16),
            pltpu.VMEM((2, 2 * up, 3 * c1), bf16),
            pltpu.VMEM((2, rows + 2 * EDGE, c1), f32),
            pltpu.VMEM((2, 2, 2 * rows, top), bf16),
            pltpu.VMEM((2, 2, rows, 2 * top), f32),
            pltpu.VMEM((2, 2, 2, rows, top), bf16),
            pltpu.VMEM((2, 2, 2, rows, deep), bf16),
            pltpu.VMEM((2, 2, 2, half, 2 * up), bf16),
            pltpu.VMEM((2, rows, 6 * c0), bf16),
            pltpu.VMEM((2, rows, k1 + c0), bf16),
            pltpu.VMEM((2, half, 3 * c1), bf16),
            pltpu.VMEM((ch // LANES, count, LANES), f32),
            pltpu.SemaphoreType.DMA((sends,)),
            pltpu.SemaphoreType.DMA((3, max(pieces), 2, members)),
            pltpu.SemaphoreType.DMA((3, TAPS)),
            pltpu.SemaphoreType.DMA((2, 5)),
            pltpu.SemaphoreType.DMA((2, 3, 8)),
        ],
        compiler_params=pltpu.CompilerParams(
            collective_id=0, has_side_effects=True, vmem_limit_bytes=67043328
        ),
    )(
        ids,
        stem_weight,
        *shards,
        gain_top,
        gain_deep,
        gain_up,
    )
    return out


def solution(mesh):
    members = mesh.shape["seq"]

    def device_step(*args):
        bases, stem_weight, weight_top, _, weight_up, *_ = args
        fits = (
            mesh.shape["groups"] == 2
            and members % 4 == 0
            and members == 16
            and weight_top.shape[2] % 16 == 0
            and weight_up.shape[2] % 16 == 0
            and stem_weight.shape[2] % 256 == 0
            and (bases.shape[0] // 2 + 2 * EDGE) % CHUNK == 0
            and bases.shape[0] % 192 == 0
            and bases.shape[0] % LANES == 0
        )
        return (fused_device if fits else per_device)(*args)

    placed = (
        P(("groups", "seq")),
        P(),
        P(None, None, "seq"),
        P(None, None, "seq"),
        P(None, None, "seq"),
        P(),
        P(),
        P(),
    )
    return jax.shard_map(
        device_step,
        mesh=mesh,
        in_specs=placed,
        out_specs=P(("groups", "seq"), None),
        check_vma=False,
    )
```

```python
import functools

import jax
import jax.numpy as jnp
from jax import lax
from jax.experimental import pallas as pl
from jax.experimental.pallas import tpu as pltpu
from jax.sharding import PartitionSpec as P

TAPS = 5


def with_halo(block, sides, width):
    for axis, dim in sides:
        count = lax.axis_size(axis)
        forward = [(i, i + 1) for i in range(count - 1)]
        backward = [(target, source) for source, target in forward]
        low = lax.ppermute(
            lax.slice_in_dim(block, block.shape[dim] - width, None, axis=dim), axis, forward
        )
        high = lax.ppermute(lax.slice_in_dim(block, 0, width, axis=dim), axis, backward)
        block = jnp.concatenate([low, block, high], axis=dim)
    return block


def activate(values, gain):
    wide = values.astype(jnp.float32)
    meansq = jnp.mean(wide * wide, axis=-1, keepdims=True)
    return jax.nn.gelu(wide * lax.rsqrt(meansq + 1e-06) * gain).astype(jnp.bfloat16)


def taps_conv(padded, weight):
    count = padded.shape[0] - weight.shape[0] + 1
    total = jnp.zeros((count, weight.shape[2]), jnp.float32)
    for tap in range(weight.shape[0]):
        total = total + jnp.dot(
            padded[tap : tap + count], weight[tap], preferred_element_type=jnp.float32
        )
    return total


def stem_embed(extended, stem_weight, count):
    window = jnp.stack([extended[tap : tap + count] for tap in range(TAPS)], axis=1)
    codes = jnp.arange(1, 5, dtype=jnp.int32)
    onehot = (
        (window[:, :, None] == codes[None, None, :]).astype(jnp.bfloat16).reshape(count, TAPS * 4)
    )
    table = stem_weight.reshape(TAPS * 4, stem_weight.shape[2])
    return jnp.dot(onehot, table, preferred_element_type=jnp.float32)


def per_device(
    bases, stem_weight, weight_top, weight_deep, weight_up, gain_top, gain_deep, gain_up
):
    count = bases.shape[0]
    half = count // 2
    full_top = lax.all_gather(weight_top, "seq", axis=2, tiled=True)
    extended = with_halo(bases + 1, (("seq", 0),), 2)
    embedded = stem_embed(extended, stem_weight, count).astype(jnp.bfloat16)
    act_top = with_halo(activate(embedded, gain_top), (("seq", 0),), 2)
    full_deep = lax.all_gather(weight_deep, "seq", axis=2, tiled=True)
    conv_top = taps_conv(act_top, full_top)
    skip = (embedded.astype(jnp.float32) + conv_top).astype(jnp.bfloat16)
    pooled = jnp.max(skip.reshape(half, 2, skip.shape[1]), axis=1)
    act_deep = with_halo(activate(pooled, gain_deep), (("seq", 0),), 2)
    full_up = lax.all_gather(weight_up, "seq", axis=2, tiled=True)
    conv_deep = taps_conv(act_deep, full_deep)
    widened = jnp.pad(
        pooled.astype(jnp.float32), ((0, 0), (0, conv_deep.shape[1] - pooled.shape[1]))
    )
    deep = (conv_deep + widened).astype(jnp.bfloat16)
    act_up = activate(deep, gain_up)
    raised = with_halo(jnp.repeat(act_up, 2, axis=0), (("seq", 0),), 2)
    conv_up = taps_conv(raised, full_up)
    return (conv_up + skip.astype(jnp.float32)).astype(jnp.bfloat16)


MESH = pl.DeviceIdType.MESH
EDGE = 8
CHUNK = 80
LANES = 128
PARTS = (2, 1, 1)
ORDER = (
    "zT", "tab", "f010", "e00", "e01", "e02", "e03", "f011", "e04", "s00", "f021", "s01", "s02",
    "s03", "cT", "s04", "e10", "z1e", "e11", "e12", "e13", "e14", "f030", "m010", "s10", "m011",
    "s11", "s12", "s13", "f031", "s14", "nT0", "tn0", "f020", "z1i", "m021", "z2e", "tn1",
    "m031", "c2", "m030", "m020", "f110", "nT1", "tf0", "f120", "tf1", "c1", "m110", "f130",
    "nD0", "z2i", "pd0", "dn0", "pd1", "f210", "dn1", "m130", "m120", "f220", "nD1", "df1",
    "df0", "m210", "f230", "nU0", "au1", "up10", "m220", "au0", "m230", "up00", "nU1", "up11",
    "up01", "end0", "end1",
)


def fused_kernel(
    nz,
    half,
    ids_in,
    stem_in,
    top_ref,
    deep_ref,
    up_ref,
    gain_top_in,
    gain_deep_in,
    gain_up_in,
    out_ref,
    ids_all,
    ids_wide,
    table,
    table_half,
    full_top,
    full_deep,
    full_up,
    flat_deep,
    both_up,
    wide,
    embedded,
    skip,
    pooled,
    deep,
    result,
    cols_top,
    cols_deep,
    cols_up,
    mixed,
    send_sem,
    recv_sem,
    own_sem,
    ids_sem,
    pair_sem,
    ids_ref,
    stem_ref,
    gain_top_ref,
    gain_deep_ref,
    gain_up_ref,
    small_sem,
):
    g = lax.axis_index("groups")
    s = lax.axis_index("seq")
    core, y, z = s % 2, (s // 2) % 2, s // 4
    members = 4 * nz
    rows = half + 2 * EDGE
    c0 = table.shape[1]
    ch = c0 // 2
    own_refs = (top_ref, deep_ref, up_ref)
    taps_in = tuple(ref.shape[2] for ref in own_refs)
    depths = tuple(ref.shape[1] for ref in own_refs)
    widths = (full_top.shape[1] // 2, full_deep.shape[2] // 2, full_up.shape[1] // 2)
    parts = []
    for width, count in zip(widths, PARTS):
        cuts = [width // LANES * n // count * LANES for n in range(count + 1)]
        parts.append([(low, high - low) for low, high in zip(cuts, cuts[1:])])
    c1 = taps_in[2]

    def index(z_at, y_at, core_at):
        return z_at * 4 + y_at * 2 + core_at

    nearest = [
        sorted(range(nz), key=lambda other: (abs(other - here), other // 2 != here // 2))
        for here in range(nz)
    ]

    def away(k):
        found = jnp.int32(0)
        for here in range(nz):
            found = jnp.where(z == here, nearest[here][k], found)
        return found

    inner = (z > 0) & (z < nz - 1)
    steps = ((z < nz - 1, 1), (z > 0, -1))

    mirror = (1 - g, s)
    across = (g, index(z, 1 - y, core))
    sibling = (g, index(z, y, 1 - core))

    def whole_rows(stage, at):
        n = (at // 4) * 2 + at % 2
        if stage == 1:
            return full_deep.at[n]
        depth = depths[stage]
        ref = full_top if stage == 0 else full_up
        return ref.at[pl.ds(pl.multiple_of(n * depth, 16), depth)]

    small = [
        pltpu.make_async_copy(source, target, small_sem.at[n])
        for n, (source, target) in enumerate(
            (
                (ids_in, ids_ref),
                (stem_in, stem_ref),
                (gain_top_in, gain_top_ref),
                (gain_deep_in, gain_deep_ref),
                (gain_up_in, gain_up_ref),
            )
        )
    ]
    for copy in small:
        copy.start()
    own_copies = []
    for stage in range(3):
        copies = []
        for tap in range(TAPS):
            width = taps_in[stage]
            copy = pltpu.make_async_copy(
                own_refs[stage].at[tap],
                whole_rows(stage, s).at[:, pl.ds(tap * width, width)],
                own_sem.at[stage, tap],
            )
            copy.start()
            copies.append(copy)
        own_copies.append(copies)

    def paired(at):
        return index(at // 4, 1 - (at // 2) % 2, at % 2)

    def inside(at):
        return (at >= 0) & (at < members)

    def device(at):
        return (g, jnp.clip(at, 0, members - 1))

    other = paired(s)
    ids_targets = [
        (s + 1, s + 1, 0),
        (s - 1, s - 1, 2),
        (paired(s + 1), s + 1, 0),
        (paired(s - 1), s - 1, 2),
        (other, s, 1),
    ]
    partners = [(mirror, True), (across, True), (sibling, True)]
    partners += [(device(at), inside(block)) for at, block, _ in ids_targets[:4]]
    partners += [(device(at), inside(at)) for at in (other - 1, other + 1)]
    partners += [
        ((g, index(jnp.clip(z + step, 0, nz - 1), y, core)), within)
        for within, step in steps
    ]
    barrier = pltpu.get_barrier_semaphore()
    count = 0
    for partner, when in partners:
        signal = functools.partial(
            pl.semaphore_signal, barrier, inc=1, device_id=partner, device_id_type=MESH
        )
        if when is True:
            signal()
            count = count + 1
        else:
            pl.when(when)(signal)
            count = count + when.astype(jnp.int32)
    pl.semaphore_wait(barrier, count)

    for copy in small:
        copy.wait()
    ids_moves = []
    for n, (target, block, slot) in enumerate(ids_targets):
        when = inside(block)
        copy = pltpu.make_async_remote_copy(
            src_ref=ids_ref,
            dst_ref=ids_all.at[jnp.clip(block, 0, members - 1) // 2 % 2, slot],
            send_sem=ids_sem.at[0, n],
            recv_sem=ids_sem.at[1, n],
            device_id=device(target),
            device_id_type=MESH,
        )
        pl.when(when)(copy.start)
        ids_moves.append((copy, when))
    ids_all[y, 1] = ids_ref[...]

    def ids_ready():
        arriving = (
            inside(s - 1),
            inside(s + 1),
            inside(other - 1),
            inside(other + 1),
            other >= 0,
        )
        for (copy, when), comes in zip(ids_moves, arriving):
            pl.when(when)(copy.wait_send)
            pl.when(comes)(copy.wait_recv)

    def place(stage, part, h, at):
        low, width = parts[stage][part]
        cols = pl.ds(pl.multiple_of(h * widths[stage] + low, LANES), width)
        return whole_rows(stage, at).at[:, cols]

    started = []

    def send(stage, part, h, at, device, when=True):
        copy = pltpu.make_async_remote_copy(
            src_ref=place(stage, part, h, at),
            dst_ref=place(stage, part, h, at),
            send_sem=send_sem.at[len(started)],
            recv_sem=recv_sem.at[stage, part, h, at],
            device_id=device,
            device_id_type=MESH,
        )
        started.append((copy, when))
        if when is True:
            copy.start()
        else:
            pl.when(when)(copy.start)

    def arrive(stage, part, h, at):
        pltpu.make_async_remote_copy(
            src_ref=place(stage, part, h, at),
            dst_ref=place(stage, part, h, at),
            send_sem=send_sem.at[0],
            recv_sem=recv_sem.at[stage, part, h, at],
            device_id=sibling,
            device_id_type=MESH,
        ).wait_recv()

    def every(stage):
        return range(len(parts[stage]))

    ready = set()

    def loaded(stage):
        if stage not in ready:
            ready.add(stage)
            for copy in own_copies[stage]:
                copy.wait()

    def along_z(stage, which=None):
        loaded(stage)
        for part in every(stage):
            for within, step in steps:
                target = (g, index(jnp.clip(z + step, 0, nz - 1), y, core))
                when = within if which is None else within & which
                send(stage, part, g, s, target, when=when)

    def own_sibling(stage):
        loaded(stage)
        for part in every(stage):
            for h in (g, 1 - g):
                send(stage, part, h, s, sibling)

    def first(stage, k, part):
        far = away(k)
        at = index(far, y, core)
        arrive(stage, part, g, at)
        onward = jnp.where(far < z, z + 1, z - 1)
        send(
            stage,
            part,
            g,
            at,
            (g, index(jnp.clip(onward, 0, nz - 1), y, core)),
            when=(onward >= 0) & (onward < nz),
        )
        send(stage, part, g, at, mirror)
        send(stage, part, g, at, sibling)

    def mirrored(stage, k, part):
        at = index(away(k), y, core)
        arrive(stage, part, 1 - g, at)
        send(stage, part, 1 - g, at, sibling)

    def need(stage, ks):
        loaded(stage)
        for h in (0, 1):
            for k in ks:
                for part in every(stage):
                    arrive(stage, part, h, index(away(k), y, 1 - core))

    chunks = range(0, rows, CHUNK)

    def act_rows(values, gain_ref, start, block):
        meansq = jnp.mean(values * values, axis=-1, keepdims=True)
        result = jax.nn.gelu(values * lax.rsqrt(meansq + 1e-06) * gain_ref[...])
        at = lax.broadcasted_iota(jnp.int32, (values.shape[0], 1), 0) + (
            block * half + start - EDGE
        )
        inside = (at >= 0) & (at < members * half)
        return jnp.where(inside, result, 0.0)

    def member_of(block):
        return index(z, block, core)

    group_top, group_deep, group_up = (4 * depth for depth in depths)

    def prepare_table():
        table[...] = jnp.zeros_like(table)
        for tap in range(TAPS):
            table[tap * 8 : tap * 8 + 4, :] = stem_ref[tap].astype(jnp.float32)
        block = c0 // members * 2
        channel = lax.broadcasted_iota(jnp.int32, (c0, ch), 0)
        local = lax.broadcasted_iota(jnp.int32, (c0, ch), 1)
        wanted = (local // block) * 2 * block + y * block + local % block
        chosen = (channel == wanted).astype(jnp.float32).astype(jnp.bfloat16)
        table_half[...] = jnp.dot(
            table[...].astype(jnp.bfloat16), chosen, preferred_element_type=jnp.float32
        ).astype(jnp.bfloat16)
        wide[...] = jnp.zeros_like(wide)
        across_rows = lax.broadcasted_iota(jnp.int32, (group_deep, c0), 0)
        channel = lax.broadcasted_iota(jnp.int32, (group_deep, c0), 1)
        block = 2 * depths[1]
        for pair in range(2):
            at = (pair * 2 + across_rows // block) * 2 * block + y * block
            same = channel == at + across_rows % block
            flat_deep[pair, :, TAPS * c0 :] = same.astype(jnp.float32).astype(jnp.bfloat16)

    def prepare_ids():
        ids_ready()
        count = 2 * half // LANES
        for block in range(2):
            at = member_of(block)
            for j in range(count + 2):
                if j == 0:
                    row = jnp.where(at > 0, ids_all[block, 0, count - 1 : count, :], 4)
                elif j <= count:
                    row = ids_all[block, 1, j - 1 : j, :]
                else:
                    row = jnp.where(at < members - 1, ids_all[block, 2, 0:1, :], 4)
                ids_wide[block, j * LANES : (j + 1) * LANES, :] = jnp.broadcast_to(
                    row.astype(jnp.float32), (LANES, LANES)
                ).T

    def window(block, parity, start):
        lane = lax.broadcasted_iota(jnp.int32, (CHUNK, LANES), 1)
        picked = jnp.full((CHUNK, LANES), 4.0, jnp.float32)
        for tap in range(TAPS):
            low = LANES + 2 * (start - EDGE) + parity + tap - 2
            moved = ids_wide[block, pl.ds(low, CHUNK, stride=2), :]
            picked = jnp.where(lane // 8 == tap, moved, picked)
        code = jnp.where(lane % 8 < 4, lane % 8, -1).astype(jnp.float32)
        return (picked == code).astype(jnp.float32).astype(jnp.bfloat16)

    def embed(block, start):
        for parity in range(2):
            hot = window(block, parity, start)
            at = parity * rows + start
            local = jnp.dot(
                hot, table_half[...], preferred_element_type=jnp.float32
            ).astype(jnp.bfloat16)
            for pair in range(2):
                embedded[pair, block, at : at + CHUNK, :] = local[
                    :, pair * group_top : (pair + 1) * group_top
                ]
            value = jnp.dot(
                hot, table[...].astype(jnp.bfloat16), preferred_element_type=jnp.float32
            ).astype(jnp.bfloat16)
            result = act_rows(
                value.astype(jnp.float32), gain_top_ref, start, member_of(block)
            )
            wide[parity, EDGE + start : EDGE + start + CHUNK, :c0] = result
            cols_top[
                block, start : start + CHUNK, (2 + parity) * c0 : (3 + parity) * c0
            ] = result.astype(jnp.bfloat16)

    def shift(block, start):
        for parity in range(2):
            for slot, step in ((0, -1), (4, 1)):
                low = EDGE + start + step
                cols_top[
                    block,
                    start : start + CHUNK,
                    (slot + parity) * c0 : (slot + parity + 1) * c0,
                ] = wide[parity, low : low + CHUNK, :c0].astype(jnp.bfloat16)

    def dot_nt(a, b):
        return lax.dot_general(
            a, b, (((1,), (1,)), ((), ())), preferred_element_type=jnp.float32
        )

    near = z // 2
    pairs = (near, 1 - near)
    exchanged = []

    def exchange(stage, n, source, target, when=True):
        copy = pltpu.make_async_remote_copy(
            src_ref=source,
            dst_ref=target,
            send_sem=pair_sem.at[0, stage, n],
            recv_sem=pair_sem.at[1, stage, n],
            device_id=across,
            device_id_type=MESH,
        )
        exchanged.append((copy, when))
        if when is True:
            copy.start()
        else:
            pl.when(when)(copy.start)

    def received(stage, n, target):
        pltpu.make_async_remote_copy(
            src_ref=target,
            dst_ref=target,
            send_sem=pair_sem.at[0, stage, n],
            recv_sem=pair_sem.at[1, stage, n],
            device_id=across,
            device_id_type=MESH,
        ).wait_recv()

    def compute_top(n, block):
        pair = pairs[n]
        weight = full_top[pl.ds(pl.multiple_of(pair * group_top, 16), group_top), :]
        values = []
        for parity in range(2):
            conv = dot_nt(cols_top[block, :, parity * c0 : (parity + TAPS) * c0], weight)
            at = slice(parity * rows, (parity + 1) * rows)
            value = embedded[pair, block, at, :].astype(jnp.float32) + conv
            value = value.astype(jnp.bfloat16).astype(jnp.float32)
            skip[pair, block, :, parity * group_top : (parity + 1) * group_top] = value
            values.append(value)
        pooled[y, pair, block] = jnp.maximum(*values).astype(jnp.bfloat16)
        ref = pooled.at[y, pair, block]
        exchange(0, 2 * n + block, ref, ref)

    def natural(ref, block, start, count, width):
        pieces = []
        for pair in range(2):
            lines = [
                ref[line, pair, block, start : start + count, :].astype(jnp.float32)
                for line in range(2)
            ]
            for low in (0, width):
                pieces += [value[:, low : low + width] for value in lines]
        return jnp.concatenate(pieces, axis=1)

    def prepare_deep(block):
        for n in range(2):
            received(0, 2 * n + block, pooled.at[1 - y, pairs[n], block])
        for start in chunks:
            value = natural(pooled, block, start, CHUNK, group_top // 2)
            cols_deep[block, start : start + CHUNK, TAPS * c0 :] = value.astype(jnp.bfloat16)
            wide[0, EDGE + start : EDGE + start + CHUNK, :c0] = act_rows(
                value, gain_deep_ref, start, member_of(block)
            )
        for start in chunks:
            for tap in range(TAPS):
                low = EDGE + start + tap - 2
                cols_deep[block, start : start + CHUNK, tap * c0 : (tap + 1) * c0] = wide[
                    0, low : low + CHUNK, :c0
                ].astype(jnp.bfloat16)

    def flatten(n):
        depth = depths[1]
        for m in range(4):
            flat_deep[pairs[n], m * depth : (m + 1) * depth, : TAPS * c0] = full_deep[
                pairs[n] * 4 + m
            ]

    def compute_deep(n, block):
        conv = dot_nt(cols_deep[block], flat_deep[pairs[n]])
        deep[y, pairs[n], block] = conv.astype(jnp.bfloat16)
        ref = deep.at[y, pairs[n], block]
        exchange(1, 2 * n + block, ref, ref)

    def prepare_up(block):
        for n in range(2):
            received(1, 2 * n + block, deep.at[1 - y, pairs[n], block])
        for start in chunks:
            value = natural(deep, block, start, CHUNK, group_deep // 2)
            wide[1, EDGE + start : EDGE + start + CHUNK, :] = act_rows(
                value, gain_up_ref, start, member_of(block)
            )
        for start in range(0, half, 96):
            for tap in range(3):
                low = 2 * EDGE + start + tap - 1
                cols_up[block, start : start + 96, tap * c1 : (tap + 1) * c1] = wide[
                    1, low : low + 96, :
                ].astype(jnp.bfloat16)

    def sum_taps(n):
        pair = pairs[n]

        @pl.loop(0, group_up // 16)
        def _(part):
            at = pl.ds(pl.multiple_of(pair * group_up + part * 16, 16), 16)
            taps = [
                full_up[at, tap * c1 : (tap + 1) * c1].astype(jnp.float32)
                for tap in range(TAPS)
            ]
            evens = (taps[0] + taps[1], taps[2] + taps[3], taps[4])
            odds = (taps[0], taps[1] + taps[2], taps[3] + taps[4])
            for parity, sums in enumerate((evens, odds)):
                to = pl.ds(pl.multiple_of(parity * group_up + part * 16, 16), 16)
                for k in range(3):
                    both_up[pair, to, k * c1 : (k + 1) * c1] = sums[k].astype(jnp.bfloat16)

    def compute_up(n, block):
        pair = pairs[n]
        part = half // 2
        for m in range(2):
            at = slice(m * part, (m + 1) * part)
            conv = dot_nt(cols_up[block, at, :], both_up[pair])
            value = conv + skip[pair, block, EDGE + m * part : EDGE + (m + 1) * part, :]
            result[y, block, pair, at, :] = value.astype(jnp.bfloat16)
            ref = result.at[y, block, pair, pl.ds(m * part, part)]
            exchange(2, 4 * block + 2 * n + m, ref, ref, when=y != block)

    def finish(n):
        part = half // 2
        pair = pairs[n]
        for block in range(2):
            for m in range(2):
                ref = result.at[1 - y, block, pair, pl.ds(m * part, part)]
                pl.when(y == block)(
                    functools.partial(received, 2, 4 * block + 2 * n + m, ref)
                )
        width = group_up // 2
        tiles = c0 // 2 // LANES
        for parity in range(2):
            low = parity * group_up
            value = jnp.concatenate(
                [
                    result[
                        line, y, pair, :, low + piece * width : low + (piece + 1) * width
                    ].astype(jnp.float32)
                    for piece in range(2)
                    for line in range(2)
                ],
                axis=1,
            )
            for tile in range(tiles):
                mixed[tile, pl.ds(parity, half, stride=2), :] = value[
                    :, tile * LANES : (tile + 1) * LANES
                ]
        for tile in range(tiles):
            low = pl.multiple_of((pair * tiles + tile) * LANES, LANES)
            out_ref[:, pl.ds(low, LANES)] = mixed[tile].astype(jnp.bfloat16)

    ends = jnp.logical_not(inner)
    others = range(1, nz)
    todo = {
        "tab": lambda: (prepare_table(), prepare_ids()),
        "zT": lambda: along_z(0),
        "cT": lambda: own_sibling(0),
        "c1": lambda: own_sibling(1),
        "c2": lambda: own_sibling(2),
        "z1e": lambda: along_z(1, ends),
        "z1i": lambda: along_z(1, inner),
        "z2e": lambda: along_z(2, ends),
        "z2i": lambda: along_z(2, inner),
        "nT0": lambda: need(0, [0, 1]),
        "nT1": lambda: need(0, others[1:]),
        "nD0": lambda: (need(1, [0, 1]), flatten(0)),
        "nD1": lambda: (need(1, others[1:]), flatten(1)),
        "nU0": lambda: (need(2, [0, 1]), sum_taps(0)),
        "nU1": lambda: (need(2, others[1:]), sum_taps(1)),
        "end0": lambda: finish(0),
        "end1": lambda: finish(1),
    }
    for b in range(2):
        for i, start in enumerate(chunks):
            todo[f"e{b}{i}"] = functools.partial(embed, b, start)
            todo[f"s{b}{i}"] = functools.partial(shift, b, start)
        for n, letter in enumerate("nf"):
            todo[f"t{letter}{b}"] = functools.partial(compute_top, n, b)
            todo[f"d{letter}{b}"] = functools.partial(compute_deep, n, b)
            todo[f"up{b}{n}"] = functools.partial(compute_up, n, b)
        todo[f"pd{b}"] = functools.partial(prepare_deep, b)
        todo[f"au{b}"] = functools.partial(prepare_up, b)
    for stage in range(3):
        for k in others:
            for part in every(stage):
                todo[f"f{stage}{k}{part}"] = functools.partial(first, stage, k, part)
                todo[f"m{stage}{k}{part}"] = functools.partial(mirrored, stage, k, part)
    for name in ORDER:
        todo.pop(name)()
    assert not todo
    for copy, when in started + exchanged:
        if when is True:
            copy.wait_send()
        else:
            pl.when(when)(copy.wait_send)


def fused_device(
    bases, stem_weight, weight_top, weight_deep, weight_up, gain_top, gain_deep, gain_up
):
    count = bases.shape[0]
    half = count // 2
    rows = half + 2 * EDGE
    members = lax.axis_size("seq")
    nz = members // 4
    c0 = stem_weight.shape[2]
    c1 = weight_up.shape[1]
    ch = c0 // 2
    bf16, f32 = jnp.bfloat16, jnp.float32

    shards = [weight.transpose(0, 2, 1) for weight in (weight_top, weight_deep, weight_up)]
    ids = bases.reshape(-1, LANES)

    k0, k1, k2 = (TAPS * shard.shape[2] for shard in shards)
    k2 += -k2 % 256
    line = members // 2
    top, deep, up = (4 * shard.shape[1] for shard in shards)
    pieces = PARTS
    sends = sum(pieces) * (4 + 2 + (nz - 1) * 4)
    out = pl.pallas_call(
        functools.partial(fused_kernel, nz, half),
        out_shape=jax.ShapeDtypeStruct((count, c0), bf16),
        in_specs=[pl.BlockSpec(memory_space=pltpu.HBM)] * 8,
        out_specs=pl.BlockSpec(memory_space=pltpu.VMEM),
        scratch_shapes=[
            pltpu.VMEM((2, 3) + ids.shape, jnp.int32),
            pltpu.VMEM((2, count + 2 * LANES, LANES), f32),
            pltpu.VMEM((LANES, c0), f32),
            pltpu.VMEM((LANES, ch), bf16),
            pltpu.VMEM((ch, k0), bf16),
            pltpu.VMEM((line, weight_deep.shape[2], k1), bf16),
            pltpu.VMEM((ch, k2), bf16),
            pltpu.VMEM((2, deep, k1 + c0), bf16),
            pltpu.VMEM((2, 2 * up, 3 * c1), bf16),
            pltpu.VMEM((2, rows + 2 * EDGE, c1), f32),
            pltpu.VMEM((2, 2, 2 * rows, top), bf16),
            pltpu.VMEM((2, 2, rows, 2 * top), f32),
            pltpu.VMEM((2, 2, 2, rows, top), bf16),
            pltpu.VMEM((2, 2, 2, rows, deep), bf16),
            pltpu.VMEM((2, 2, 2, half, 2 * up), bf16),
            pltpu.VMEM((2, rows, 6 * c0), bf16),
            pltpu.VMEM((2, rows, k1 + c0), bf16),
            pltpu.VMEM((2, half, 3 * c1), bf16),
            pltpu.VMEM((ch // LANES, count, LANES), f32),
            pltpu.SemaphoreType.DMA((sends,)),
            pltpu.SemaphoreType.DMA((3, max(pieces), 2, members)),
            pltpu.SemaphoreType.DMA((3, TAPS)),
            pltpu.SemaphoreType.DMA((2, 5)),
            pltpu.SemaphoreType.DMA((2, 3, 8)),
            pltpu.VMEM(ids.shape, jnp.int32),
            pltpu.VMEM(stem_weight.shape, bf16),
            pltpu.VMEM(gain_top.shape, f32),
            pltpu.VMEM(gain_deep.shape, f32),
            pltpu.VMEM(gain_up.shape, f32),
            pltpu.SemaphoreType.DMA((5,)),
        ],
        compiler_params=pltpu.CompilerParams(
            collective_id=0, has_side_effects=True, vmem_limit_bytes=67043328
        ),
    )(
        ids,
        stem_weight,
        *shards,
        gain_top,
        gain_deep,
        gain_up,
    )
    return out


def solution(mesh):
    members = mesh.shape["seq"]

    def device_step(*args):
        bases, stem_weight, weight_top, _, weight_up, *_ = args
        fits = (
            mesh.shape["groups"] == 2
            and members % 4 == 0
            and members == 16
            and weight_top.shape[2] % 16 == 0
            and weight_up.shape[2] % 16 == 0
            and stem_weight.shape[2] % 256 == 0
            and (bases.shape[0] // 2 + 2 * EDGE) % CHUNK == 0
            and bases.shape[0] % 192 == 0
            and bases.shape[0] % LANES == 0
        )
        return (fused_device if fits else per_device)(*args)

    placed = (
        P(("groups", "seq")),
        P(),
        P(None, None, "seq"),
        P(None, None, "seq"),
        P(None, None, "seq"),
        P(),
        P(),
        P(),
    )
    return jax.shard_map(
        device_step,
        mesh=mesh,
        in_specs=placed,
        out_specs=P(("groups", "seq"), None),
        check_vma=False,
    )
```

```python
import functools

import jax
import jax.numpy as jnp
from jax import lax
from jax.experimental import pallas as pl
from jax.experimental.pallas import tpu as pltpu
from jax.sharding import PartitionSpec as P

TAPS = 5


def with_halo(block, sides, width):
    for axis, dim in sides:
        count = lax.axis_size(axis)
        forward = [(i, i + 1) for i in range(count - 1)]
        backward = [(target, source) for source, target in forward]
        low = lax.ppermute(
            lax.slice_in_dim(block, block.shape[dim] - width, None, axis=dim), axis, forward
        )
        high = lax.ppermute(lax.slice_in_dim(block, 0, width, axis=dim), axis, backward)
        block = jnp.concatenate([low, block, high], axis=dim)
    return block


def activate(values, gain):
    wide = values.astype(jnp.float32)
    meansq = jnp.mean(wide * wide, axis=-1, keepdims=True)
    return jax.nn.gelu(wide * lax.rsqrt(meansq + 1e-06) * gain).astype(jnp.bfloat16)


def taps_conv(padded, weight):
    count = padded.shape[0] - weight.shape[0] + 1
    total = jnp.zeros((count, weight.shape[2]), jnp.float32)
    for tap in range(weight.shape[0]):
        total = total + jnp.dot(
            padded[tap : tap + count], weight[tap], preferred_element_type=jnp.float32
        )
    return total


def stem_embed(extended, stem_weight, count):
    window = jnp.stack([extended[tap : tap + count] for tap in range(TAPS)], axis=1)
    codes = jnp.arange(1, 5, dtype=jnp.int32)
    onehot = (
        (window[:, :, None] == codes[None, None, :]).astype(jnp.bfloat16).reshape(count, TAPS * 4)
    )
    table = stem_weight.reshape(TAPS * 4, stem_weight.shape[2])
    return jnp.dot(onehot, table, preferred_element_type=jnp.float32)


def per_device(
    bases, stem_weight, weight_top, weight_deep, weight_up, gain_top, gain_deep, gain_up
):
    count = bases.shape[0]
    half = count // 2
    full_top = lax.all_gather(weight_top, "seq", axis=2, tiled=True)
    extended = with_halo(bases + 1, (("seq", 0),), 2)
    embedded = stem_embed(extended, stem_weight, count).astype(jnp.bfloat16)
    act_top = with_halo(activate(embedded, gain_top), (("seq", 0),), 2)
    full_deep = lax.all_gather(weight_deep, "seq", axis=2, tiled=True)
    conv_top = taps_conv(act_top, full_top)
    skip = (embedded.astype(jnp.float32) + conv_top).astype(jnp.bfloat16)
    pooled = jnp.max(skip.reshape(half, 2, skip.shape[1]), axis=1)
    act_deep = with_halo(activate(pooled, gain_deep), (("seq", 0),), 2)
    full_up = lax.all_gather(weight_up, "seq", axis=2, tiled=True)
    conv_deep = taps_conv(act_deep, full_deep)
    widened = jnp.pad(
        pooled.astype(jnp.float32), ((0, 0), (0, conv_deep.shape[1] - pooled.shape[1]))
    )
    deep = (conv_deep + widened).astype(jnp.bfloat16)
    act_up = activate(deep, gain_up)
    raised = with_halo(jnp.repeat(act_up, 2, axis=0), (("seq", 0),), 2)
    conv_up = taps_conv(raised, full_up)
    return (conv_up + skip.astype(jnp.float32)).astype(jnp.bfloat16)


MESH = pl.DeviceIdType.MESH
EDGE = 8
CHUNK = 80
LANES = 128
PARTS = (2, 1, 1)
ORDER = (
    "zT", "tab", "f010", "e00", "e01", "e02", "e03", "f011", "e04", "s00", "f021", "s01", "s02",
    "s03", "cT", "s04", "e10", "z1e", "e11", "e12", "e13", "e14", "f030", "m010", "s10", "m011",
    "s11", "s12", "s13", "f031", "s14", "nT0", "tn0", "f020", "z1i", "m021", "z2e", "tn1",
    "m031", "c2", "m030", "m020", "f110", "nT1", "tf0", "f120", "tf1", "c1", "m110", "f130",
    "nD0", "z2i", "pd0", "dn0", "pd1", "f210", "dn1", "m130", "m120", "f220", "nD1", "df1",
    "df0", "m210", "f230", "nU0", "au1", "up10", "m220", "au0", "m230", "up00", "nU1", "up11",
    "up01", "end0", "end1",
)


def fused_kernel(
    nz,
    half,
    ids_in,
    stem_in,
    top_ref,
    deep_ref,
    up_ref,
    gain_top_in,
    gain_deep_in,
    gain_up_in,
    out_ref,
    ids_all,
    ids_wide,
    table,
    table_half,
    full_top,
    full_deep,
    full_up,
    flat_deep,
    both_up,
    wide,
    embedded,
    skip,
    pooled,
    packed,
    deep,
    result,
    cols_top,
    cols_deep,
    cols_up,
    mixed,
    send_sem,
    recv_sem,
    own_sem,
    ids_sem,
    pair_sem,
    ids_ref,
    stem_ref,
    gain_top_ref,
    gain_deep_ref,
    gain_up_ref,
    small_sem,
):
    g = lax.axis_index("groups")
    s = lax.axis_index("seq")
    core, y, z = s % 2, (s // 2) % 2, s // 4
    members = 4 * nz
    rows = half + 2 * EDGE
    c0 = table.shape[1]
    ch = c0 // 2
    own_refs = (top_ref, deep_ref, up_ref)
    taps_in = tuple(ref.shape[2] for ref in own_refs)
    depths = tuple(ref.shape[1] for ref in own_refs)
    widths = (full_top.shape[1] // 2, full_deep.shape[2] // 2, full_up.shape[1] // 2)
    parts = []
    for width, count in zip(widths, PARTS):
        cuts = [width // LANES * n // count * LANES for n in range(count + 1)]
        parts.append([(low, high - low) for low, high in zip(cuts, cuts[1:])])
    c1 = taps_in[2]

    def index(z_at, y_at, core_at):
        return z_at * 4 + y_at * 2 + core_at

    nearest = [
        sorted(range(nz), key=lambda other: (abs(other - here), other // 2 != here // 2))
        for here in range(nz)
    ]

    def away(k):
        found = jnp.int32(0)
        for here in range(nz):
            found = jnp.where(z == here, nearest[here][k], found)
        return found

    inner = (z > 0) & (z < nz - 1)
    steps = ((z < nz - 1, 1), (z > 0, -1))

    mirror = (1 - g, s)
    across = (g, index(z, 1 - y, core))
    sibling = (g, index(z, y, 1 - core))

    def whole_rows(stage, at):
        n = (at // 4) * 2 + at % 2
        if stage == 1:
            return full_deep.at[n]
        depth = depths[stage]
        ref = full_top if stage == 0 else full_up
        return ref.at[pl.ds(pl.multiple_of(n * depth, 16), depth)]

    small = [
        pltpu.make_async_copy(source, target, small_sem.at[n])
        for n, (source, target) in enumerate(
            (
                (ids_in, ids_ref),
                (stem_in, stem_ref),
                (gain_top_in, gain_top_ref),
                (gain_deep_in, gain_deep_ref),
                (gain_up_in, gain_up_ref),
            )
        )
    ]
    for copy in small:
        copy.start()
    own_copies = []
    for stage in range(3):
        copies = []
        for tap in range(TAPS):
            width = taps_in[stage]
            copy = pltpu.make_async_copy(
                own_refs[stage].at[tap],
                whole_rows(stage, s).at[:, pl.ds(tap * width, width)],
                own_sem.at[stage, tap],
            )
            copy.start()
            copies.append(copy)
        own_copies.append(copies)

    def paired(at):
        return index(at // 4, 1 - (at // 2) % 2, at % 2)

    def inside(at):
        return (at >= 0) & (at < members)

    def device(at):
        return (g, jnp.clip(at, 0, members - 1))

    other = paired(s)
    ids_targets = [
        (s + 1, s + 1, 0),
        (s - 1, s - 1, 2),
        (paired(s + 1), s + 1, 0),
        (paired(s - 1), s - 1, 2),
        (other, s, 1),
    ]
    partners = [(mirror, True), (across, True), (sibling, True)]
    partners += [(device(at), inside(block)) for at, block, _ in ids_targets[:4]]
    partners += [(device(at), inside(at)) for at in (other - 1, other + 1)]
    partners += [
        ((g, index(jnp.clip(z + step, 0, nz - 1), y, core)), within)
        for within, step in steps
    ]
    barrier = pltpu.get_barrier_semaphore()
    count = 0
    for partner, when in partners:
        signal = functools.partial(
            pl.semaphore_signal, barrier, inc=1, device_id=partner, device_id_type=MESH
        )
        if when is True:
            signal()
            count = count + 1
        else:
            pl.when(when)(signal)
            count = count + when.astype(jnp.int32)
    pl.semaphore_wait(barrier, count)

    for copy in small:
        copy.wait()
    ids_moves = []
    for n, (target, block, slot) in enumerate(ids_targets):
        when = inside(block)
        copy = pltpu.make_async_remote_copy(
            src_ref=ids_ref,
            dst_ref=ids_all.at[jnp.clip(block, 0, members - 1) // 2 % 2, slot],
            send_sem=ids_sem.at[0, n],
            recv_sem=ids_sem.at[1, n],
            device_id=device(target),
            device_id_type=MESH,
        )
        pl.when(when)(copy.start)
        ids_moves.append((copy, when))
    ids_all[y, 1] = ids_ref[...]

    def ids_ready():
        arriving = (
            inside(s - 1),
            inside(s + 1),
            inside(other - 1),
            inside(other + 1),
            other >= 0,
        )
        for (copy, when), comes in zip(ids_moves, arriving):
            pl.when(when)(copy.wait_send)
            pl.when(comes)(copy.wait_recv)

    def place(stage, part, h, at):
        low, width = parts[stage][part]
        cols = pl.ds(pl.multiple_of(h * widths[stage] + low, LANES), width)
        return whole_rows(stage, at).at[:, cols]

    started = []

    def send(stage, part, h, at, device, when=True):
        copy = pltpu.make_async_remote_copy(
            src_ref=place(stage, part, h, at),
            dst_ref=place(stage, part, h, at),
            send_sem=send_sem.at[len(started)],
            recv_sem=recv_sem.at[stage, part, h, at],
            device_id=device,
            device_id_type=MESH,
        )
        started.append((copy, when))
        if when is True:
            copy.start()
        else:
            pl.when(when)(copy.start)

    def arrive(stage, part, h, at):
        pltpu.make_async_remote_copy(
            src_ref=place(stage, part, h, at),
            dst_ref=place(stage, part, h, at),
            send_sem=send_sem.at[0],
            recv_sem=recv_sem.at[stage, part, h, at],
            device_id=sibling,
            device_id_type=MESH,
        ).wait_recv()

    def every(stage):
        return range(len(parts[stage]))

    ready = set()

    def loaded(stage):
        if stage not in ready:
            ready.add(stage)
            for copy in own_copies[stage]:
                copy.wait()

    def along_z(stage, which=None):
        loaded(stage)
        for part in every(stage):
            for within, step in steps:
                target = (g, index(jnp.clip(z + step, 0, nz - 1), y, core))
                when = within if which is None else within & which
                send(stage, part, g, s, target, when=when)

    def own_sibling(stage):
        loaded(stage)
        for part in every(stage):
            for h in (g, 1 - g):
                send(stage, part, h, s, sibling)

    def first(stage, k, part):
        far = away(k)
        at = index(far, y, core)
        arrive(stage, part, g, at)
        onward = jnp.where(far < z, z + 1, z - 1)
        send(
            stage,
            part,
            g,
            at,
            (g, index(jnp.clip(onward, 0, nz - 1), y, core)),
            when=(onward >= 0) & (onward < nz),
        )
        send(stage, part, g, at, mirror)
        send(stage, part, g, at, sibling)

    def mirrored(stage, k, part):
        at = index(away(k), y, core)
        arrive(stage, part, 1 - g, at)
        send(stage, part, 1 - g, at, sibling)

    def need(stage, ks):
        loaded(stage)
        for h in (0, 1):
            for k in ks:
                for part in every(stage):
                    arrive(stage, part, h, index(away(k), y, 1 - core))

    chunks = range(0, rows, CHUNK)

    def act_rows(values, gain_ref, start, block):
        meansq = jnp.mean(values * values, axis=-1, keepdims=True)
        result = jax.nn.gelu(values * lax.rsqrt(meansq + 1e-06) * gain_ref[...])
        at = lax.broadcasted_iota(jnp.int32, (values.shape[0], 1), 0) + (
            block * half + start - EDGE
        )
        inside = (at >= 0) & (at < members * half)
        return jnp.where(inside, result, 0.0)

    def member_of(block):
        return index(z, block, core)

    group_top, group_deep, group_up = (4 * depth for depth in depths)

    def prepare_table():
        table[...] = jnp.zeros_like(table)
        for tap in range(TAPS):
            table[tap * 8 : tap * 8 + 4, :] = stem_ref[tap].astype(jnp.float32)
        block = c0 // members * 2
        channel = lax.broadcasted_iota(jnp.int32, (c0, ch), 0)
        local = lax.broadcasted_iota(jnp.int32, (c0, ch), 1)
        wanted = (local // block) * 2 * block + y * block + local % block
        chosen = (channel == wanted).astype(jnp.float32).astype(jnp.bfloat16)
        table_half[...] = jnp.dot(
            table[...].astype(jnp.bfloat16), chosen, preferred_element_type=jnp.float32
        ).astype(jnp.bfloat16)
        wide[...] = jnp.zeros_like(wide)
        across_rows = lax.broadcasted_iota(jnp.int32, (group_deep, c0), 0)
        channel = lax.broadcasted_iota(jnp.int32, (group_deep, c0), 1)
        block = 2 * depths[1]
        for pair in range(2):
            at = (pair * 2 + across_rows // block) * 2 * block + y * block
            same = channel == at + across_rows % block
            flat_deep[pair, :, TAPS * c0 :] = same.astype(jnp.float32).astype(jnp.bfloat16)

    def prepare_ids():
        ids_ready()
        count = 2 * half // LANES
        for block in range(2):
            at = member_of(block)
            for j in range(count + 2):
                if j == 0:
                    row = jnp.where(at > 0, ids_all[block, 0, count - 1 : count, :], 4)
                elif j <= count:
                    row = ids_all[block, 1, j - 1 : j, :]
                else:
                    row = jnp.where(at < members - 1, ids_all[block, 2, 0:1, :], 4)
                ids_wide[block, j * LANES : (j + 1) * LANES, :] = jnp.broadcast_to(
                    row.astype(jnp.float32), (LANES, LANES)
                ).T

    def window(block, parity, start):
        lane = lax.broadcasted_iota(jnp.int32, (CHUNK, LANES), 1)
        picked = jnp.full((CHUNK, LANES), 4.0, jnp.float32)
        for tap in range(TAPS):
            low = LANES + 2 * (start - EDGE) + parity + tap - 2
            moved = ids_wide[block, pl.ds(low, CHUNK, stride=2), :]
            picked = jnp.where(lane // 8 == tap, moved, picked)
        code = jnp.where(lane % 8 < 4, lane % 8, -1).astype(jnp.float32)
        return (picked == code).astype(jnp.float32).astype(jnp.bfloat16)

    def embed(block, start):
        for parity in range(2):
            hot = window(block, parity, start)
            at = parity * rows + start
            local = jnp.dot(
                hot, table_half[...], preferred_element_type=jnp.float32
            ).astype(jnp.bfloat16)
            for pair in range(2):
                embedded[pair, block, at : at + CHUNK, :] = local[
                    :, pair * group_top : (pair + 1) * group_top
                ]
            value = jnp.dot(
                hot, table[...].astype(jnp.bfloat16), preferred_element_type=jnp.float32
            ).astype(jnp.bfloat16)
            result = act_rows(
                value.astype(jnp.float32), gain_top_ref, start, member_of(block)
            )
            wide[parity, EDGE + start : EDGE + start + CHUNK, :c0] = result
            cols_top[
                block, start : start + CHUNK, (2 + parity) * c0 : (3 + parity) * c0
            ] = result.astype(jnp.bfloat16)

    def shift(block, start):
        for parity in range(2):
            for slot, step in ((0, -1), (4, 1)):
                low = EDGE + start + step
                cols_top[
                    block,
                    start : start + CHUNK,
                    (slot + parity) * c0 : (slot + parity + 1) * c0,
                ] = wide[parity, low : low + CHUNK, :c0].astype(jnp.bfloat16)

    def dot_nt(a, b):
        return lax.dot_general(
            a, b, (((1,), (1,)), ((), ())), preferred_element_type=jnp.float32
        )

    near = z // 2
    pairs = (near, 1 - near)
    exchanged = []

    def exchange(stage, n, source, target, when=True):
        copy = pltpu.make_async_remote_copy(
            src_ref=source,
            dst_ref=target,
            send_sem=pair_sem.at[0, stage, n],
            recv_sem=pair_sem.at[1, stage, n],
            device_id=across,
            device_id_type=MESH,
        )
        exchanged.append((copy, when))
        if when is True:
            copy.start()
        else:
            pl.when(when)(copy.start)

    def received(stage, n, target):
        pltpu.make_async_remote_copy(
            src_ref=target,
            dst_ref=target,
            send_sem=pair_sem.at[0, stage, n],
            recv_sem=pair_sem.at[1, stage, n],
            device_id=across,
            device_id_type=MESH,
        ).wait_recv()

    def compute_top(n, block):
        pair = pairs[n]
        weight = full_top[pl.ds(pl.multiple_of(pair * group_top, 16), group_top), :]
        values = []
        for parity in range(2):
            conv = dot_nt(cols_top[block, :, parity * c0 : (parity + TAPS) * c0], weight)
            at = slice(parity * rows, (parity + 1) * rows)
            value = embedded[pair, block, at, :].astype(jnp.float32) + conv
            value = value.astype(jnp.bfloat16).astype(jnp.float32)
            skip[pair, block, :, parity * group_top : (parity + 1) * group_top] = value
            values.append(value)
        value = jnp.maximum(*values).astype(jnp.bfloat16)
        rest = group_top - LANES
        if n == 0:
            pooled[y, block] = value[:, :LANES]
            packed[y, block, :, :rest] = value[:, LANES:]
            ref = pooled.at[y, block]
        else:
            packed[y, block, :, rest:] = value
            ref = packed.at[y, block]
        exchange(0, 2 * n + block, ref, ref)

    def pooled_pairs(line, block, start):
        at = slice(start, start + CHUNK)
        rest = group_top - LANES
        tail = packed[line, block, at, :].astype(jnp.float32)
        head = pooled[line, block, at, :].astype(jnp.float32)
        closer = jnp.concatenate([head, tail[:, :rest]], axis=1)
        farther = tail[:, rest:]
        return [jnp.where(near == pair, closer, farther) for pair in range(2)]

    def deep_pairs(line, block, start):
        return [
            deep[line, pair, block, start : start + CHUNK, :].astype(jnp.float32)
            for pair in range(2)
        ]

    def natural(read, block, start, width):
        lines = [read(line, block, start) for line in range(2)]
        return jnp.concatenate(
            [
                lines[line][pair][:, low : low + width]
                for pair in range(2)
                for low in (0, width)
                for line in range(2)
            ],
            axis=1,
        )

    def prepare_deep(block):
        for n in range(2):
            received(0, 2 * n + block, (pooled, packed)[n].at[1 - y, block])
        for start in chunks:
            value = natural(pooled_pairs, block, start, group_top // 2)
            cols_deep[block, start : start + CHUNK, TAPS * c0 :] = value.astype(jnp.bfloat16)
            wide[0, EDGE + start : EDGE + start + CHUNK, :c0] = act_rows(
                value, gain_deep_ref, start, member_of(block)
            )
        for start in chunks:
            for tap in range(TAPS):
                low = EDGE + start + tap - 2
                cols_deep[block, start : start + CHUNK, tap * c0 : (tap + 1) * c0] = wide[
                    0, low : low + CHUNK, :c0
                ].astype(jnp.bfloat16)

    def flatten(n):
        depth = depths[1]
        for m in range(4):
            flat_deep[pairs[n], m * depth : (m + 1) * depth, : TAPS * c0] = full_deep[
                pairs[n] * 4 + m
            ]

    def compute_deep(n, block):
        conv = dot_nt(cols_deep[block], flat_deep[pairs[n]])
        deep[y, pairs[n], block] = conv.astype(jnp.bfloat16)
        ref = deep.at[y, pairs[n], block]
        exchange(1, 2 * n + block, ref, ref)

    def prepare_up(block):
        for n in range(2):
            received(1, 2 * n + block, deep.at[1 - y, pairs[n], block])
        for start in chunks:
            value = natural(deep_pairs, block, start, group_deep // 2)
            wide[1, EDGE + start : EDGE + start + CHUNK, :] = act_rows(
                value, gain_up_ref, start, member_of(block)
            )
        for start in range(0, half, 96):
            for tap in range(3):
                low = 2 * EDGE + start + tap - 1
                cols_up[block, start : start + 96, tap * c1 : (tap + 1) * c1] = wide[
                    1, low : low + 96, :
                ].astype(jnp.bfloat16)

    def sum_taps(n):
        pair = pairs[n]

        @pl.loop(0, group_up // 16)
        def _(part):
            at = pl.ds(pl.multiple_of(pair * group_up + part * 16, 16), 16)
            taps = [
                full_up[at, tap * c1 : (tap + 1) * c1].astype(jnp.float32)
                for tap in range(TAPS)
            ]
            evens = (taps[0] + taps[1], taps[2] + taps[3], taps[4])
            odds = (taps[0], taps[1] + taps[2], taps[3] + taps[4])
            for parity, sums in enumerate((evens, odds)):
                to = pl.ds(pl.multiple_of(parity * group_up + part * 16, 16), 16)
                for k in range(3):
                    both_up[pair, to, k * c1 : (k + 1) * c1] = sums[k].astype(jnp.bfloat16)

    def compute_up(n, block):
        pair = pairs[n]
        part = half // 2
        for m in range(2):
            at = slice(m * part, (m + 1) * part)
            conv = dot_nt(cols_up[block, at, :], both_up[pair])
            value = conv + skip[pair, block, EDGE + m * part : EDGE + (m + 1) * part, :]
            result[y, block, pair, at, :] = value.astype(jnp.bfloat16)
            ref = result.at[y, block, pair, pl.ds(m * part, part)]
            exchange(2, 4 * block + 2 * n + m, ref, ref, when=y != block)

    def finish(n):
        part = half // 2
        pair = pairs[n]
        for block in range(2):
            for m in range(2):
                ref = result.at[1 - y, block, pair, pl.ds(m * part, part)]
                pl.when(y == block)(
                    functools.partial(received, 2, 4 * block + 2 * n + m, ref)
                )
        width = group_up // 2
        tiles = c0 // 2 // LANES
        for parity in range(2):
            low = parity * group_up
            value = jnp.concatenate(
                [
                    result[
                        line, y, pair, :, low + piece * width : low + (piece + 1) * width
                    ].astype(jnp.float32)
                    for piece in range(2)
                    for line in range(2)
                ],
                axis=1,
            )
            for tile in range(tiles):
                mixed[tile, pl.ds(parity, half, stride=2), :] = value[
                    :, tile * LANES : (tile + 1) * LANES
                ]
        for tile in range(tiles):
            low = pl.multiple_of((pair * tiles + tile) * LANES, LANES)
            out_ref[:, pl.ds(low, LANES)] = mixed[tile].astype(jnp.bfloat16)

    ends = jnp.logical_not(inner)
    others = range(1, nz)
    todo = {
        "tab": lambda: (prepare_table(), prepare_ids()),
        "zT": lambda: along_z(0),
        "cT": lambda: own_sibling(0),
        "c1": lambda: own_sibling(1),
        "c2": lambda: own_sibling(2),
        "z1e": lambda: along_z(1, ends),
        "z1i": lambda: along_z(1, inner),
        "z2e": lambda: along_z(2, ends),
        "z2i": lambda: along_z(2, inner),
        "nT0": lambda: need(0, [0, 1]),
        "nT1": lambda: need(0, others[1:]),
        "nD0": lambda: (need(1, [0, 1]), flatten(0)),
        "nD1": lambda: (need(1, others[1:]), flatten(1)),
        "nU0": lambda: (need(2, [0, 1]), sum_taps(0)),
        "nU1": lambda: (need(2, others[1:]), sum_taps(1)),
        "end0": lambda: finish(0),
        "end1": lambda: finish(1),
    }
    for b in range(2):
        for i, start in enumerate(chunks):
            todo[f"e{b}{i}"] = functools.partial(embed, b, start)
            todo[f"s{b}{i}"] = functools.partial(shift, b, start)
        for n, letter in enumerate("nf"):
            todo[f"t{letter}{b}"] = functools.partial(compute_top, n, b)
            todo[f"d{letter}{b}"] = functools.partial(compute_deep, n, b)
            todo[f"up{b}{n}"] = functools.partial(compute_up, n, b)
        todo[f"pd{b}"] = functools.partial(prepare_deep, b)
        todo[f"au{b}"] = functools.partial(prepare_up, b)
    for stage in range(3):
        for k in others:
            for part in every(stage):
                todo[f"f{stage}{k}{part}"] = functools.partial(first, stage, k, part)
                todo[f"m{stage}{k}{part}"] = functools.partial(mirrored, stage, k, part)
    for name in ORDER:
        todo.pop(name)()
    assert not todo
    for copy, when in started + exchanged:
        if when is True:
            copy.wait_send()
        else:
            pl.when(when)(copy.wait_send)


def fused_device(
    bases, stem_weight, weight_top, weight_deep, weight_up, gain_top, gain_deep, gain_up
):
    count = bases.shape[0]
    half = count // 2
    rows = half + 2 * EDGE
    members = lax.axis_size("seq")
    nz = members // 4
    c0 = stem_weight.shape[2]
    c1 = weight_up.shape[1]
    ch = c0 // 2
    bf16, f32 = jnp.bfloat16, jnp.float32

    shards = [weight.transpose(0, 2, 1) for weight in (weight_top, weight_deep, weight_up)]
    ids = bases.reshape(-1, LANES)

    k0, k1, k2 = (TAPS * shard.shape[2] for shard in shards)
    k2 += -k2 % 256
    line = members // 2
    top, deep, up = (4 * shard.shape[1] for shard in shards)
    pieces = PARTS
    sends = sum(pieces) * (4 + 2 + (nz - 1) * 4)
    out = pl.pallas_call(
        functools.partial(fused_kernel, nz, half),
        out_shape=jax.ShapeDtypeStruct((count, c0), bf16),
        in_specs=[pl.BlockSpec(memory_space=pltpu.HBM)] * 8,
        out_specs=pl.BlockSpec(memory_space=pltpu.VMEM),
        scratch_shapes=[
            pltpu.VMEM((2, 3) + ids.shape, jnp.int32),
            pltpu.VMEM((2, count + 2 * LANES, LANES), f32),
            pltpu.VMEM((LANES, c0), f32),
            pltpu.VMEM((LANES, ch), bf16),
            pltpu.VMEM((ch, k0), bf16),
            pltpu.VMEM((line, weight_deep.shape[2], k1), bf16),
            pltpu.VMEM((ch, k2), bf16),
            pltpu.VMEM((2, deep, k1 + c0), bf16),
            pltpu.VMEM((2, 2 * up, 3 * c1), bf16),
            pltpu.VMEM((2, rows + 2 * EDGE, c1), f32),
            pltpu.VMEM((2, 2, 2 * rows, top), bf16),
            pltpu.VMEM((2, 2, rows, 2 * top), f32),
            pltpu.VMEM((2, 2, rows, LANES), bf16),
            pltpu.VMEM((2, 2, rows, 2 * top - LANES), bf16),
            pltpu.VMEM((2, 2, 2, rows, deep), bf16),
            pltpu.VMEM((2, 2, 2, half, 2 * up), bf16),
            pltpu.VMEM((2, rows, 6 * c0), bf16),
            pltpu.VMEM((2, rows, k1 + c0), bf16),
            pltpu.VMEM((2, half, 3 * c1), bf16),
            pltpu.VMEM((ch // LANES, count, LANES), f32),
            pltpu.SemaphoreType.DMA((sends,)),
            pltpu.SemaphoreType.DMA((3, max(pieces), 2, members)),
            pltpu.SemaphoreType.DMA((3, TAPS)),
            pltpu.SemaphoreType.DMA((2, 5)),
            pltpu.SemaphoreType.DMA((2, 3, 8)),
            pltpu.VMEM(ids.shape, jnp.int32),
            pltpu.VMEM(stem_weight.shape, bf16),
            pltpu.VMEM(gain_top.shape, f32),
            pltpu.VMEM(gain_deep.shape, f32),
            pltpu.VMEM(gain_up.shape, f32),
            pltpu.SemaphoreType.DMA((5,)),
        ],
        compiler_params=pltpu.CompilerParams(
            collective_id=0, has_side_effects=True, vmem_limit_bytes=67043328
        ),
    )(
        ids,
        stem_weight,
        *shards,
        gain_top,
        gain_deep,
        gain_up,
    )
    return out


def solution(mesh):
    members = mesh.shape["seq"]

    def device_step(*args):
        bases, stem_weight, weight_top, _, weight_up, *_ = args
        fits = (
            mesh.shape["groups"] == 2
            and members % 4 == 0
            and members == 16
            and weight_top.shape[2] % 16 == 0
            and weight_up.shape[2] % 16 == 0
            and stem_weight.shape[2] % 256 == 0
            and (bases.shape[0] // 2 + 2 * EDGE) % CHUNK == 0
            and bases.shape[0] % 192 == 0
            and bases.shape[0] % LANES == 0
        )
        return (fused_device if fits else per_device)(*args)

    placed = (
        P(("groups", "seq")),
        P(),
        P(None, None, "seq"),
        P(None, None, "seq"),
        P(None, None, "seq"),
        P(),
        P(),
        P(),
    )
    return jax.shard_map(
        device_step,
        mesh=mesh,
        in_specs=placed,
        out_specs=P(("groups", "seq"), None),
        check_vma=False,
    )
```
